32 devices in a mesh: blk: 8 (over y, x, core), walk: 4 (over z).
Axes of the slice: x: 2, y: 2, z: 4, core: 2. Of those that a mesh axis runs over, the one named last changes fastest.
Arguments:
- walkers: bfloat16 [64, 200, 2048], P(('blk', 'walk')), may hold values from -6 to 6
- inv_intersection: bfloat16 [64, 2, 100, 100], P(('blk', 'walk')), may hold values from -0.625 to 0.625
- rotated_chol: bfloat16 [16, 100, 2048], P('blk'), may hold values from -0.013671875 to 0.013671875
- full_chol: bfloat16 [16, 2048, 2048], P('walk', 'blk'), may hold values from -0.125 to 0.125
- field_noise: float32 [16], replicated, may hold values from -4 to 4
Outputs:
- propagated: bfloat16 [64, 200, 2048], P(('blk', 'walk'))
- force_bias: float32 [64, 16], P(('blk', 'walk'))
- bias_shift: float32 [16], replicated
The draws below stay inside these ranges and needn't reach their ends.
All inputs are finite; a program needn't handle non-finite values.
Results may differ from the reference program's by a relative error of at most 0.0065.
Values may be sent and summed in bfloat16 or wider, within the bound.
A program may use at most 128 MiB of HBM per device.

```python
import jax
import jax.numpy as jnp
from jax import lax

NORB = 2048
NOCC = 100
WALKERS = 64
CHOL = 16


def block_levels(stream_key, shape, split, least, top_value):
    loudness = 1.0
    for position, parts in split:
        draws = jax.random.uniform(jax.random.fold_in(jax.random.fold_in(stream_key, 6), position), (parts,), jnp.float32, least / len(split), top_value / len(split))
        loudness = loudness * jnp.repeat(jnp.exp(draws), shape[position] // parts).reshape((-1,) + (1,) * (len(shape) - 1 - position))
    return loudness


def scatter_about(own_key, extent, scale, reach, cuts=(), dtype=jnp.bfloat16):
    factor_of = block_levels(own_key, extent, cuts, -0.22, 0.18) if cuts else 1.0
    array = jax.random.normal(own_key, extent, jnp.float32) * scale * factor_of
    return jnp.minimum(jnp.maximum(array, -reach), reach).astype(dtype)


def setup_inputs(seed: int = 0) -> dict:
    splits = jax.random.split(jax.random.key(seed), 6)
    return {
        "walkers": scatter_about(splits[0], (WALKERS, 2 * NOCC, NORB), 1.0, 6.0, ((0, 32),)),
        "inv_intersection": scatter_about(splits[1], (WALKERS, 2, NOCC, NOCC), NOCC ** -0.5, 0.625, ((0, 32),)),
        "rotated_chol": scatter_about(splits[2], (CHOL, NOCC, NORB), (NOCC * NORB) ** -0.5, 0.013671875, ((0, 8),)),
        "full_chol": scatter_about(splits[3], (CHOL, NORB, NORB), NORB ** -0.5, 0.125, ((0, 4), (1, 8))),
        "field_noise": scatter_about(splits[4], (CHOL,), 1.0, 4.0, (), jnp.float32),
    }


def reference(walkers, inv_intersection, rotated_chol, full_chol, field_noise):
    spins = walkers.reshape(WALKERS, 2, NOCC, NORB)
    theta = jnp.einsum('wsij,wsjp->wip', inv_intersection.astype(jnp.float32), spins.astype(jnp.float32)).astype(jnp.bfloat16)
    force_bias = jnp.einsum('wip,gip->wg', theta.astype(jnp.float32), rotated_chol.astype(jnp.float32))
    bias_shift = lax.optimization_barrier(jnp.sum(force_bias, axis=0)) / jnp.sqrt(jnp.float32(WALKERS))
    shifted = field_noise - bias_shift
    field = 0.1 * jnp.einsum('g,gij->ij', shifted, full_chol.astype(jnp.float32), precision=lax.Precision.HIGHEST)
    field = field.astype(jnp.bfloat16)
    current = walkers.reshape(WALKERS * 2 * NOCC, NORB)
    total = current.astype(jnp.float32)
    for order in range(1, 5):
        current = (jnp.dot(current, field, preferred_element_type=jnp.float32) / order).astype(jnp.bfloat16)
        total = total + current.astype(jnp.float32)
    propagated = total.astype(jnp.bfloat16).reshape(WALKERS, 2 * NOCC, NORB)
    return (propagated, force_bias, bias_shift)
```

```python
import functools
import math

import jax
import jax.numpy as jnp
from jax import lax
from jax.experimental import pallas as pl
from jax.experimental.pallas import tpu as pltpu
from jax.sharding import PartitionSpec as P

time_root = 0.1
orders = 4
f32, bf16 = jnp.float32, jnp.bfloat16
MESH = pl.DeviceIdType.MESH


class Gather:
    def __init__(self, nb, ref_at, recv, send_f, send_s, send_w, send_b):
        self.nb, self.ref_at, self.recv = nb, ref_at, recv
        self.send_f, self.send_s, self.send_w, self.send_b = send_f, send_s, send_w, send_b
        me = lax.axis_index("blk")
        self.me, self.core = me, me % 2
        self.cols = 2 if nb % 4 == 0 else 1
        self.rows = nb // 2 // self.cols
        chip = me // 2
        col, row = chip % self.cols, chip // self.cols
        self.turn = self.core if self.rows == self.cols else 0
        self.f = (1 - self.turn) * col + self.turn * row
        self.s = (1 - self.turn) * row + self.turn * col
        self.nf, self.ns = self.cols, self.rows
        self.sibling = chip * 2 + 1 - self.core

    def at(self, i, j):
        f, s = (self.f + i) % self.nf, (self.s + j) % self.ns
        chip = (1 - self.turn) * (s * self.cols + f) + self.turn * (f * self.cols + s)
        return chip * 2 + self.core

    def copy(self, block, chunk, target, send):
        piece = self.ref_at(block, chunk)
        return pltpu.make_async_remote_copy(
            src_ref=piece, dst_ref=piece, send_sem=send, recv_sem=self.recv.at[block, chunk],
            device_id=target if isinstance(target, dict) else {"blk": target}, device_id_type=MESH)

    def landed(self, block, chunk):
        self.copy(block, chunk, self.sibling, self.send_b).wait_recv()

    def own(self, chunk):
        for i in range(1, self.nf):
            self.copy(self.me, chunk, self.at(i, 0), self.send_f).start()
        for j in range(1, self.ns):
            self.copy(self.me, chunk, self.at(0, j), self.send_s).start()
        self.copy(self.me, chunk, self.sibling, self.send_b).start()

    def first(self, chunk, forward):
        for i in range(1, self.nf):
            block = self.at(i, 0)
            self.landed(block, chunk)

            @pl.when(forward)
            def _():
                for j in range(1, self.ns):
                    self.copy(block, chunk, self.at(0, j), self.send_w).start()

            self.copy(block, chunk, self.sibling, self.send_b).start()

    def second(self, chunk, relayed):
        for j in range(1, self.ns):
            for i in range(self.nf):
                block = self.at(i, j)
                self.landed(block, chunk)
                if i and relayed is not None:
                    relayed(block)
                self.copy(block, chunk, self.sibling, self.send_b).start()


def kernel(nb, nw, total_walkers, chunks, parts, every, flat_hbm, three_hbm, inv_hbm, rot_hbm, full_hbm, noise_hbm,
           field, last, partial, fb, shift,
           flat, three, inv_raw, inv, noise, own_rot, rots, full, theta, thetas, pair, mine, zout, zin,
           spread_rows, wide, sums, fb_out, fb_in, mid, outer_in, inner_in, slots_w, slots_b, terms,
           fld_recv, fld_f, fld_s, fld_w, fld_b, fld_r,
           load, slot_send, slot_recv, in_send, in_recv, mid_send, mid_recv, out_send, out_recv):
    blk, walk = lax.axis_index("blk"), lax.axis_index("walk")
    wdev, occupied, orbitals = theta.shape
    per, tiles = rots.shape[3], rots.shape[2]
    group = nb * per
    slab = tiles * 128
    local_count, block_rows = full.shape[0], full.shape[1]
    size = orbitals // chunks

    loads = [pltpu.make_async_copy(src, dst, load.at[k]) for k, (src, dst) in enumerate((
        (inv_hbm, inv_raw), (three_hbm, three), (rot_hbm, own_rot), (noise_hbm, noise), (flat_hbm, flat), (full_hbm, full)))]
    for one in loads:
        one.start()
    load_inv, load_three, load_rot, load_noise, load_flat, load_full = loads
    barrier = pltpu.get_barrier_semaphore()
    for d in range(1, nb):
        pl.semaphore_signal(barrier, inc=1, device_id={"blk": (blk + d) % nb}, device_id_type=MESH)
    for d in range(1, nw):
        pl.semaphore_signal(barrier, inc=1, device_id={"walk": (walk + d) % nw}, device_id_type=MESH)

    def one_hot(shape, wanted):
        row, column = lax.broadcasted_iota(jnp.int32, shape, 0), lax.broadcasted_iota(jnp.int32, shape, 1)
        return jnp.where(wanted(row, column), 1.0, 0.0).astype(bf16)

    load_inv.wait()
    for w in range(wdev):
        whole = jnp.zeros((occupied, 2 * occupied), f32)
        for s in range(2):
            take = one_hot((occupied, inv_raw.shape[0]), lambda r, c: c == 2 * (r + w * occupied) + s)
            place = one_hot((occupied, 2 * occupied), lambda r, c: c == r + s * occupied)
            block = jnp.dot(take, inv_raw[...], preferred_element_type=f32).astype(bf16)
            whole = whole + jnp.dot(block, place, preferred_element_type=f32)
        inv[w] = whole.astype(bf16)
    for t in range(tiles):
        spread_rows[t] = one_hot(spread_rows.shape[1:],
                                 lambda r, c: (r >= (c * tiles + t) * per) & (r < (c * tiles + t + 1) * per))

    load_three.wait()
    load_rot.wait()
    pl.semaphore_wait(barrier, nb + nw - 2)

    def slab_of(b, z):
        return (b % 2) * nw + (b // 2 + z) % nw if parts == 2 else (b + z) % nw

    slab_columns = lambda s: pl.ds(pl.multiple_of(s * slab, slab), slab)
    home = slab_of(blk, walk)
    sibling = blk // 2 * 2 + 1 - blk % 2
    walk_peers = [({"walk": (walk + d) % nw}, (walk + d) % nw) for d in range(1, nw)]
    blk_peers = [({"blk": (blk + d) % nb}, (blk + d) % nb) for d in range(1, nb)]

    def share(slots, source_at, me, peers, k):
        for peer, slot in peers:
            pltpu.make_async_remote_copy(
                src_ref=source_at(slot), dst_ref=slots.at[me],
                send_sem=slot_send.at[k], recv_sem=slot_recv.at[k], device_id=peer, device_id_type=MESH).start()

        def finish():
            rest = slots.at[pl.ds(0, len(peers))]
            pltpu.make_async_remote_copy(
                src_ref=rest, dst_ref=rest, send_sem=slot_send.at[k], recv_sem=slot_recv.at[k],
                device_id=peers[0][0], device_id_type=MESH).wait()

        return finish

    rot_slab = lambda b: own_rot.at[:, pl.ds(slab_of(b, walk) * tiles, tiles)]
    rots_arrive = share(rots, rot_slab, blk, blk_peers, 0)
    keep_rot = pltpu.make_async_copy(rot_slab(blk), rots.at[blk], load.at[2])
    keep_rot.start()

    tile = 512
    span_width = mine.shape[1]

    def project(begin, into):
        for lo in range(0, span_width, tile):
            span = pl.ds(pl.multiple_of(begin + lo, tile), tile)
            both = jnp.zeros((occupied, tile), f32)
            for w in range(wdev):
                one = jnp.dot(inv[w], three[w, :, span], preferred_element_type=f32).astype(bf16)
                theta[w, :, span] = one
                both = both + one.astype(f32)
            into[:, lo:lo + tile] = both

    if parts == 2:
        project((1 - blk % 2) * span_width, pair.at[0])
        swap = pltpu.make_async_remote_copy(
            src_ref=pair.at[0], dst_ref=pair.at[1], send_sem=slot_send.at[4], recv_sem=slot_recv.at[4],
            device_id={"blk": sibling}, device_id_type=MESH)
        swap.start()
        project(blk % 2 * span_width, mine)
        swap.wait()
    else:
        project(0, mine)
    for k in range(nw):
        columns = slab_columns(slab_of(blk, k) % nw)
        value = mine[:, columns]
        if parts == 2:
            value = value + pair[1, :, columns]
        zout[k] = value.astype(bf16)
    zin[pl.ds(walk, 1)] = zout[pl.ds(walk, 1)]
    sums_arrive = share(zin, lambda z: zout.at[z], walk, walk_peers, 1)
    thetas_arrive = share(thetas, lambda b: theta.at[:, :, slab_columns(slab_of(b, walk))], blk, blk_peers, 2)
    thetas[pl.ds(blk, 1)] = theta[:, :, slab_columns(home)][None]

    def widen(narrow):
        value = jnp.dot(spread_rows[0], narrow[:, 0:128], preferred_element_type=f32)
        for t in range(1, tiles):
            value = value + jnp.dot(spread_rows[t], narrow[:, t * 128:(t + 1) * 128], preferred_element_type=f32)
        return value

    deep = spread_rows.shape[1]
    fold = lambda value: jnp.sum(value.reshape(deep // 8, 8, 128), axis=0)
    vectors_of = lambda b: rots.at[b].reshape(deep, 128)[...].astype(f32)
    row = lax.broadcasted_iota(jnp.int32, (nb * 8, 128), 0)
    lane = lax.broadcasted_iota(jnp.int32, (nb * 8, 128), 1)
    picked = lane == row // 8 * per + row % per

    def line_of(value):
        return jnp.sum(jnp.where(picked, jnp.sum(value, axis=1, keepdims=True), 0.0), axis=0, keepdims=True)

    sums_arrive()
    value = zin[0].astype(f32)
    for k in range(1, nw):
        value = value + zin[k].astype(f32)
    wide[0] = widen(value.astype(bf16))
    keep_rot.wait()
    rots_arrive()
    for b in range(nb):
        sums[0, b * 8:(b + 1) * 8] = fold(vectors_of(b) * wide[0])
    line = line_of(sums[0])
    for peers, me, slots, k in ((walk_peers, walk, slots_w, 5), (blk_peers, blk, slots_b, 6)):
        slots[pl.ds(me, 1)] = line[None]
        share(slots, lambda slot: slots.at[me], me, peers, k)()
        line = slots[0]
        for d in range(1, slots.shape[0]):
            line = line + slots[d]
    shifts = line / math.sqrt(total_walkers)
    shift[...] = shifts[:, 0:group]
    load_noise.wait()
    shifted = (noise[...] - shifts[:, 0:group]) * time_root
    lanes = lax.broadcasted_iota(jnp.int32, (1, group), 1)
    weights = [jnp.sum(jnp.where(lanes == walk * local_count + j, shifted, 0.0), axis=1, keepdims=True)
               for j in range(local_count)]
    load_full.wait()
    load_flat.wait()

    half = nw // 2
    is_mid = (walk == half - 1) | (walk == half)
    has_outer = (walk != 0) & (walk != nw - 1)
    step = 1 - 2 * (walk >= half).astype(jnp.int32)
    inward = (walk + step + nw) % nw
    outward = (walk - step + nw) % nw
    outer_lag = min(8, chunks)
    lag = jnp.where(is_mid, 2, outer_lag)
    cols = lambda c: pl.ds(pl.multiple_of(c * size, size), size)
    rows = lambda block: pl.ds(pl.multiple_of(block * block_rows, block_rows), block_rows)
    part_at = lambda block, c: field.at[rows(block), cols(c)]
    gather = Gather(nb, part_at, fld_recv, fld_f, fld_s, fld_w, fld_b)

    def hop(src, dst, send, recv, target):
        return pltpu.make_async_remote_copy(src_ref=src, dst_ref=dst, send_sem=send, recv_sem=recv,
                                            device_id={"walk": target}, device_id_type=MESH)

    def to_mid(c):
        return hop(mid.at[c], outer_in.at[c], in_send, in_recv.at[c], inward)

    def across(c):
        return hop(mid.at[c], inner_in.at[c], mid_send, mid_recv.at[c], inward)

    def back(c):
        return hop(part_at(blk, c), part_at(blk, c), out_send, out_recv.at[c], outward)

    def reduce_in(c):
        value = weights[0] * full[0, :, cols(c)].astype(f32)
        for j in range(1, local_count):
            value = value + weights[j] * full[j, :, cols(c)].astype(f32)

        @pl.when(has_outer)
        def _():
            to_mid(c).wait_recv()
            mid[c] = (value + outer_in[c].astype(f32)).astype(bf16)

        @pl.when(jnp.logical_not(has_outer))
        def _():
            mid[c] = value.astype(bf16)

        @pl.when(is_mid)
        def _():
            across(c).start()

        @pl.when(jnp.logical_not(is_mid))
        def _():
            to_mid(c).start()

    def spread(c):
        @pl.when(is_mid)
        def _():
            across(c).wait_recv()
            field[rows(blk), cols(c)] = (mid[c].astype(f32) + inner_in[c].astype(f32)).astype(bf16)

        @pl.when(jnp.logical_not(is_mid))
        def _():
            back(c).wait_recv()

        @pl.when(has_outer)
        def _():
            back(c).start()

        gather.own(c)

    by_walk = lambda c: c % every == 1
    relays = len([c for c in range(chunks) if c % every == 1]) if every else 0

    def first(c):
        gather.first(c, is_mid | jnp.logical_not(by_walk(c)) if every else c >= 0)

    def second(c):
        def relayed(block):
            @pl.when(is_mid & by_walk(c))
            def _():
                gather.copy(block, c, {"walk": outward}, fld_r).start()

        gather.second(c, relayed if every else None)

    def when_chunk(c, action):
        @pl.when((c >= 0) & (c < chunks))
        def _():
            action(c)

    def first_term(c):
        for e in range(2):
            for d in range(nb // 2):
                gather.landed((sibling + 2 * d) % nb, c - 1 + e)
        span = pl.ds(pl.multiple_of((c - 1) * size, 2 * size), 2 * size)
        terms[0, :, span] = jnp.dot(flat[...], field[:, span], preferred_element_type=f32).astype(bf16)

    def bias(b):
        for w in range(wdev):
            wide[w] = widen(thetas[b, w])

        @pl.loop(0, nb)
        def _(v):
            vectors = vectors_of(v)
            for w in range(wdev):
                sums[w, pl.ds(pl.multiple_of(v * 8, 8), 8)] = fold(vectors * wide[w])

        for w in range(wdev):
            fb_out[b, w:w + 1] = line_of(sums[w])

    @pl.loop(0, chunks + outer_lag + 6)
    def _(t):
        when_chunk(t - lag, spread)
        when_chunk(t, reduce_in)
        when_chunk(t - lag - 2, first)
        when_chunk(t - lag - 4, second)
        pl.when(t == 2)(thetas_arrive)
        when = t - 2

        @pl.when((when >= 0) & (when < nb))
        def _():
            bias(when)

        @pl.when(((t - lag - 5) % 2 == 1) & (t - lag - 5 > 0) & (t - lag - 5 < chunks))
        def _():
            first_term(t - lag - 5)

    fb_in[pl.ds(blk, 1)] = fb_out[pl.ds(blk, 1)]
    biases_arrive = share(fb_in, lambda b: fb_out.at[b], blk, blk_peers, 3)

    width = orbitals // 2
    for order in range(2, orders):
        @pl.loop(0, orbitals // width)
        def _(n):
            span = pl.ds(pl.multiple_of(n * width, width), width)
            term = (jnp.dot(terms[order - 2], field[:, span], preferred_element_type=f32) / order).astype(bf16)
            if order == orders - 1:
                value = flat[:, span].astype(f32)
                for k in range(orders - 2):
                    value = value + terms[k, :, span].astype(f32)
                partial[:, span] = value + term.astype(f32)
                last[:, span] = term
            else:
                terms[order - 1, :, span] = term

    biases_arrive()
    value = fb_in[0]
    for b in range(1, nb):
        value = value + fb_in[b]
    fb[...] = value[:, 0:group]

    def drain(piece, send):
        pltpu.make_async_remote_copy(src_ref=piece, dst_ref=piece, send_sem=send, recv_sem=fld_recv.at[0, 0],
                                     device_id={"blk": sibling}, device_id_type=MESH).wait_send()

    def many(count, send):
        if count:
            drain(field.at[pl.ds(0, count * block_rows)], send)

    many(gather.nf - 1, fld_f)
    many(gather.ns - 1, fld_s)
    many(nb // 2, fld_b)
    if every:
        @pl.when(is_mid)
        def _():
            many((gather.ns - 1) * (gather.nf - 1), fld_w)
            drain(field.at[pl.ds(0, block_rows), pl.ds(0, relays * size)], fld_r)

        @pl.when(jnp.logical_not(is_mid))
        def _():
            drain(field.at[pl.ds(0, block_rows), pl.ds(0, (chunks - relays) * size)], fld_w)
    else:
        many((gather.ns - 1) * (gather.nf - 1), fld_w)

    @pl.when(is_mid)
    def _():
        drain(mid, mid_send)

    @pl.when(jnp.logical_not(is_mid))
    def _():
        drain(mid, in_send)

    @pl.when(has_outer)
    def _():
        drain(field.at[pl.ds(0, block_rows)], out_send)


def closing(field, last, partial, fb, shift, out, fb_out, shift_out, held, sems):
    orbitals = field.shape[1]
    width = orbitals // 4
    small = [pltpu.make_async_copy(src, dst, sems.at[4 + k]) for k, (src, dst) in enumerate(((fb, fb_out), (shift, shift_out)))]
    for copy in small:
        copy.start()
    copies = []
    for n in range(4):
        span = pl.ds(n * width, width)
        term = (jnp.dot(last[...], field[:, span], preferred_element_type=f32) / orders).astype(bf16)
        held[:, span] = (partial[:, span] + term.astype(f32)).astype(bf16)
        copies.append(pltpu.make_async_copy(held.at[:, span], out.at[:, span], sems.at[n]))
        copies[-1].start()
    for copy in small + copies:
        copy.wait()


def local(nb, nw, walkers, inv_intersection, rotated_chol, full_chol, field_noise):
    wdev, double_rows, orbitals = walkers.shape
    occupied = double_rows // 2
    group = field_noise.shape[0]
    per = rotated_chol.shape[0]
    local_count, block_rows, _ = full_chol.shape
    chunks = 16
    size = orbitals // chunks
    parts = nb // nw
    assert nb == parts * nw and parts in (1, 2)
    tiles = orbitals // nb // 128
    every = 3 if nw == 4 and nb == 8 else 0
    flat = walkers.reshape(wdev * double_rows, orbitals)
    inv = inv_intersection.transpose(0, 2, 1, 3).reshape(wdev * double_rows, occupied)
    rot = rotated_chol.transpose(1, 0, 2).reshape(occupied, per, orbitals // 128, 128).transpose(0, 2, 1, 3)
    vmem, hbm = pl.BlockSpec(memory_space=pltpu.VMEM), pl.BlockSpec(memory_space=pltpu.HBM)
    dma = pltpu.SemaphoreType.DMA
    span = orbitals // parts
    results = pl.pallas_call(
        functools.partial(kernel, nb, nw, wdev * nb * nw, chunks, parts, every),
        out_shape=(pltpu.VMEM((orbitals, orbitals), bf16), pltpu.VMEM(flat.shape, bf16), pltpu.VMEM(flat.shape, f32),
                   pltpu.VMEM((wdev, group), f32), pltpu.VMEM((1, group), f32)),
        in_specs=[hbm] * 6,
        out_specs=(vmem,) * 5,
        scratch_shapes=[
            pltpu.VMEM(flat.shape, bf16),
            pltpu.VMEM(walkers.shape, bf16),
            pltpu.VMEM(inv.shape, bf16),
            pltpu.VMEM((wdev, occupied, double_rows), bf16),
            pltpu.VMEM((1, group), f32),
            pltpu.VMEM(rot.shape, bf16),
            pltpu.VMEM((nb, occupied, tiles, per, 128), bf16),
            pltpu.VMEM(full_chol.shape, bf16),
            pltpu.VMEM((wdev, occupied, orbitals), bf16),
            pltpu.VMEM((nb, wdev, occupied, tiles * 128), bf16),
            pltpu.VMEM((2, occupied, span), f32),
            pltpu.VMEM((occupied, span), f32),
            pltpu.VMEM((nw, occupied, tiles * 128), bf16),
            pltpu.VMEM((nw, occupied, tiles * 128), bf16),
            pltpu.VMEM((tiles, occupied * tiles * per, occupied), bf16),
            pltpu.VMEM((wdev, occupied * tiles * per, 128), f32),
            pltpu.VMEM((wdev, nb * 8, 128), f32),
            pltpu.VMEM((nb, wdev, 128), f32),
            pltpu.VMEM((nb, wdev, 128), f32),
            pltpu.VMEM((chunks, block_rows, size), bf16),
            pltpu.VMEM((chunks, block_rows, size), bf16),
            pltpu.VMEM((chunks, block_rows, size), bf16),
            pltpu.VMEM((nw, 1, 128), f32),
            pltpu.VMEM((nb, 1, 128), f32),
            pltpu.VMEM((orders - 2,) + flat.shape, bf16),
            dma((nb, chunks)), dma, dma, dma, dma, dma,
            dma((6,)), dma((7,)), dma((7,)),
            dma, dma((chunks,)), dma, dma((chunks,)), dma, dma((chunks,)),
        ],
        compiler_params=pltpu.CompilerParams(collective_id=0, has_side_effects=True, vmem_limit_bytes=38 * 2**20),
    )(flat, walkers, inv, rot, full_chol, field_noise.reshape(1, group))
    results = [pltpu.with_memory_space_constraint(result, pltpu.VMEM) for result in results]
    out, fb, shift = pl.pallas_call(
        closing,
        out_shape=(jax.ShapeDtypeStruct(flat.shape, bf16), jax.ShapeDtypeStruct((wdev, group), f32),
                   jax.ShapeDtypeStruct((1, group), f32)),
        in_specs=[vmem] * 5,
        out_specs=(hbm,) * 3,
        scratch_shapes=[pltpu.VMEM(flat.shape, bf16), dma((6,))],
        compiler_params=pltpu.CompilerParams(vmem_limit_bytes=16 * 2**20),
    )(*results)
    return (out.reshape(walkers.shape), fb, shift.reshape(group))


def solution(mesh):
    placed = (
        P(("blk", "walk"), None, None),
        P(("blk", "walk"), None, None, None),
        P("blk", None, None),
        P("walk", "blk", None),
        P(),
    )
    return jax.shard_map(
        functools.partial(local, mesh.shape["blk"], mesh.shape["walk"]),
        mesh=mesh,
        in_specs=placed,
        out_specs=(P(("blk", "walk"), None, None), P(("blk", "walk"), None), P()),
        check_vma=False,
    )
```

```python
import functools
import math

import jax
import jax.numpy as jnp
from jax import lax
from jax.experimental import pallas as pl
from jax.experimental.pallas import tpu as pltpu
from jax.sharding import PartitionSpec as P

time_root = 0.1
orders = 4
f32, bf16 = jnp.float32, jnp.bfloat16
MESH = pl.DeviceIdType.MESH


class Gather:
    def __init__(self, nb, ref_at, recv, send_f, send_s, send_w, send_b):
        self.nb, self.ref_at, self.recv = nb, ref_at, recv
        self.send_f, self.send_s, self.send_w, self.send_b = send_f, send_s, send_w, send_b
        me = lax.axis_index("blk")
        self.me, self.core = me, me % 2
        self.cols = 2 if nb % 4 == 0 else 1
        self.rows = nb // 2 // self.cols
        chip = me // 2
        col, row = chip % self.cols, chip // self.cols
        self.turn = self.core if self.rows == self.cols else 0
        self.f = (1 - self.turn) * col + self.turn * row
        self.s = (1 - self.turn) * row + self.turn * col
        self.nf, self.ns = self.cols, self.rows
        self.sibling = chip * 2 + 1 - self.core

    def at(self, i, j):
        f, s = (self.f + i) % self.nf, (self.s + j) % self.ns
        chip = (1 - self.turn) * (s * self.cols + f) + self.turn * (f * self.cols + s)
        return chip * 2 + self.core

    def copy(self, block, chunk, target, send):
        piece = self.ref_at(block, chunk)
        return pltpu.make_async_remote_copy(
            src_ref=piece, dst_ref=piece, send_sem=send, recv_sem=self.recv.at[block, chunk],
            device_id=target if isinstance(target, dict) else {"blk": target}, device_id_type=MESH)

    def landed(self, block, chunk):
        self.copy(block, chunk, self.sibling, self.send_b).wait_recv()

    def own(self, chunk):
        for i in range(1, self.nf):
            self.copy(self.me, chunk, self.at(i, 0), self.send_f).start()
        for j in range(1, self.ns):
            self.copy(self.me, chunk, self.at(0, j), self.send_s).start()
        self.copy(self.me, chunk, self.sibling, self.send_b).start()

    def first(self, chunk, forward):
        for i in range(1, self.nf):
            block = self.at(i, 0)
            self.landed(block, chunk)

            @pl.when(forward)
            def _():
                for j in range(1, self.ns):
                    self.copy(block, chunk, self.at(0, j), self.send_w).start()

            self.copy(block, chunk, self.sibling, self.send_b).start()

    def second(self, chunk, relayed):
        for j in range(1, self.ns):
            for i in range(self.nf):
                block = self.at(i, j)
                self.landed(block, chunk)
                if i and relayed is not None:
                    relayed(block)
                self.copy(block, chunk, self.sibling, self.send_b).start()


def kernel(nb, nw, total_walkers, chunks, parts, every, flat_hbm, three_hbm, inv_hbm, rot_hbm, full_hbm, noise_hbm,
           field, last, partial, fb, shift,
           flat, three, inv_raw, inv, noise, own_rot, rots, full, theta, thetas, pair, mine, zout, zin,
           vectors, spread_rows, wide, sums, fb_out, fb_in, mid, outer_in, inner_in, slots_w, slots_b, terms,
           fld_recv, fld_f, fld_s, fld_w, fld_b, fld_r,
           load, slot_send, slot_recv, in_send, in_recv, mid_send, mid_recv, out_send, out_recv):
    blk, walk = lax.axis_index("blk"), lax.axis_index("walk")
    wdev, occupied, orbitals = theta.shape
    per, tiles = rots.shape[3], rots.shape[2]
    group = nb * per
    slab = tiles * 128
    local_count, block_rows = full.shape[0], full.shape[1]
    size = orbitals // chunks

    loads = [pltpu.make_async_copy(src, dst, load.at[k]) for k, (src, dst) in enumerate((
        (inv_hbm, inv_raw), (three_hbm, three), (rot_hbm, own_rot), (noise_hbm, noise), (flat_hbm, flat), (full_hbm, full)))]
    for one in loads:
        one.start()
    load_inv, load_three, load_rot, load_noise, load_flat, load_full = loads
    barrier = pltpu.get_barrier_semaphore()
    for d in range(1, nb):
        pl.semaphore_signal(barrier, inc=1, device_id={"blk": (blk + d) % nb}, device_id_type=MESH)
    for d in range(1, nw):
        pl.semaphore_signal(barrier, inc=1, device_id={"walk": (walk + d) % nw}, device_id_type=MESH)

    def one_hot(shape, wanted):
        row, column = lax.broadcasted_iota(jnp.int32, shape, 0), lax.broadcasted_iota(jnp.int32, shape, 1)
        return jnp.where(wanted(row, column), 1.0, 0.0).astype(bf16)

    load_inv.wait()
    for w in range(wdev):
        whole = jnp.zeros((occupied, 2 * occupied), f32)
        for s in range(2):
            take = one_hot((occupied, inv_raw.shape[0]), lambda r, c: c == 2 * (r + w * occupied) + s)
            place = one_hot((occupied, 2 * occupied), lambda r, c: c == r + s * occupied)
            block = jnp.dot(take, inv_raw[...], preferred_element_type=f32).astype(bf16)
            whole = whole + jnp.dot(block, place, preferred_element_type=f32)
        inv[w] = whole.astype(bf16)
    for t in range(tiles):
        spread_rows[t] = one_hot(spread_rows.shape[1:],
                                 lambda r, c: (r >= (c * tiles + t) * per) & (r < (c * tiles + t + 1) * per))

    load_three.wait()
    load_rot.wait()
    pl.semaphore_wait(barrier, nb + nw - 2)

    def slab_of(b, z):
        return (b % 2) * nw + (b // 2 + z) % nw if parts == 2 else (b + z) % nw

    slab_columns = lambda s: pl.ds(pl.multiple_of(s * slab, slab), slab)
    home = slab_of(blk, walk)
    sibling = blk // 2 * 2 + 1 - blk % 2
    walk_peers = [({"walk": (walk + d) % nw}, (walk + d) % nw) for d in range(1, nw)]
    blk_peers = [({"blk": (blk + d) % nb}, (blk + d) % nb) for d in range(1, nb)]

    def share(slots, source_at, me, peers, k):
        for peer, slot in peers:
            pltpu.make_async_remote_copy(
                src_ref=source_at(slot), dst_ref=slots.at[me],
                send_sem=slot_send.at[k], recv_sem=slot_recv.at[k], device_id=peer, device_id_type=MESH).start()

        def finish():
            rest = slots.at[pl.ds(0, len(peers))]
            pltpu.make_async_remote_copy(
                src_ref=rest, dst_ref=rest, send_sem=slot_send.at[k], recv_sem=slot_recv.at[k],
                device_id=peers[0][0], device_id_type=MESH).wait()

        return finish

    rot_slab = lambda b: own_rot.at[:, pl.ds(slab_of(b, walk) * tiles, tiles)]
    rots_arrive = share(rots, rot_slab, blk, blk_peers, 0)
    keep_rot = pltpu.make_async_copy(rot_slab(blk), rots.at[blk], load.at[2])
    keep_rot.start()

    tile = 512
    span_width = mine.shape[1]

    def project(begin, into):
        for lo in range(0, span_width, tile):
            span = pl.ds(pl.multiple_of(begin + lo, tile), tile)
            both = jnp.zeros((occupied, tile), f32)
            for w in range(wdev):
                one = jnp.dot(inv[w], three[w, :, span], preferred_element_type=f32).astype(bf16)
                theta[w, :, span] = one
                both = both + one.astype(f32)
            into[:, lo:lo + tile] = both

    if parts == 2:
        project((1 - blk % 2) * span_width, pair.at[0])
        swap = pltpu.make_async_remote_copy(
            src_ref=pair.at[0], dst_ref=pair.at[1], send_sem=slot_send.at[4], recv_sem=slot_recv.at[4],
            device_id={"blk": sibling}, device_id_type=MESH)
        swap.start()
        project(blk % 2 * span_width, mine)
        swap.wait()
    else:
        project(0, mine)
    for k in range(nw):
        columns = slab_columns(slab_of(blk, k) % nw)
        value = mine[:, columns]
        if parts == 2:
            value = value + pair[1, :, columns]
        zout[k] = value.astype(bf16)
    zin[pl.ds(walk, 1)] = zout[pl.ds(walk, 1)]
    sums_arrive = share(zin, lambda z: zout.at[z], walk, walk_peers, 1)
    thetas_arrive = share(thetas, lambda b: theta.at[:, :, slab_columns(slab_of(b, walk))], blk, blk_peers, 2)
    thetas[pl.ds(blk, 1)] = theta[:, :, slab_columns(home)][None]

    def widen(narrow):
        pieces = []
        for t in range(tiles):
            side = [each[:, t * 128:(t + 1) * 128] for each in narrow]
            side = side[0] if len(side) == 1 else jnp.concatenate(side, axis=1)
            pieces.append(jnp.dot(spread_rows[t], side, preferred_element_type=f32))
        return functools.reduce(jnp.add, pieces)

    deep = spread_rows.shape[1]
    fold = lambda value: jnp.sum(value.reshape(deep // 8, 8, 128), axis=0)
    row = lax.broadcasted_iota(jnp.int32, (nb * 8, 128), 0)
    lane = lax.broadcasted_iota(jnp.int32, (nb * 8, 128), 1)
    picked = lane == row // 8 * per + row % per

    def line_of(value):
        return jnp.sum(jnp.where(picked, jnp.sum(value, axis=1, keepdims=True), 0.0), axis=0, keepdims=True)

    keep_rot.wait()
    rots_arrive()
    for b in range(nb):
        vectors[b] = rots.at[b].reshape(deep, 128)[...].astype(f32)
    sums_arrive()
    value = zin[0].astype(f32)
    for k in range(1, nw):
        value = value + zin[k].astype(f32)
    wide[:, 0:128] = widen([value.astype(bf16)])
    for b in range(nb):
        sums[0, b * 8:(b + 1) * 8] = fold(vectors[b] * wide[:, 0:128])
    line = line_of(sums[0])
    for peers, me, slots, k in ((walk_peers, walk, slots_w, 5), (blk_peers, blk, slots_b, 6)):
        slots[pl.ds(me, 1)] = line[None]
        share(slots, lambda slot: slots.at[me], me, peers, k)()
        line = slots[0]
        for d in range(1, slots.shape[0]):
            line = line + slots[d]
    shifts = line / math.sqrt(total_walkers)
    shift[...] = shifts[:, 0:group]
    load_noise.wait()
    shifted = (noise[...] - shifts[:, 0:group]) * time_root
    lanes = lax.broadcasted_iota(jnp.int32, (1, group), 1)
    weights = [jnp.sum(jnp.where(lanes == walk * local_count + j, shifted, 0.0), axis=1, keepdims=True)
               for j in range(local_count)]
    load_full.wait()
    load_flat.wait()

    half = nw // 2
    is_mid = (walk == half - 1) | (walk == half)
    has_outer = (walk != 0) & (walk != nw - 1)
    step = 1 - 2 * (walk >= half).astype(jnp.int32)
    inward = (walk + step + nw) % nw
    outward = (walk - step + nw) % nw
    outer_lag = min(8, chunks)
    lag = jnp.where(is_mid, 2, outer_lag)
    cols = lambda c: pl.ds(pl.multiple_of(c * size, size), size)
    rows = lambda block: pl.ds(pl.multiple_of(block * block_rows, block_rows), block_rows)
    part_at = lambda block, c: field.at[rows(block), cols(c)]
    gather = Gather(nb, part_at, fld_recv, fld_f, fld_s, fld_w, fld_b)

    def hop(src, dst, send, recv, target):
        return pltpu.make_async_remote_copy(src_ref=src, dst_ref=dst, send_sem=send, recv_sem=recv,
                                            device_id={"walk": target}, device_id_type=MESH)

    def to_mid(c):
        return hop(mid.at[c], outer_in.at[c], in_send, in_recv.at[c], inward)

    def across(c):
        return hop(mid.at[c], inner_in.at[c], mid_send, mid_recv.at[c], inward)

    def back(c):
        return hop(part_at(blk, c), part_at(blk, c), out_send, out_recv.at[c], outward)

    def reduce_in(c):
        value = weights[0] * full[0, :, cols(c)].astype(f32)
        for j in range(1, local_count):
            value = value + weights[j] * full[j, :, cols(c)].astype(f32)

        @pl.when(has_outer)
        def _():
            to_mid(c).wait_recv()
            mid[c] = (value + outer_in[c].astype(f32)).astype(bf16)

        @pl.when(jnp.logical_not(has_outer))
        def _():
            mid[c] = value.astype(bf16)

        @pl.when(is_mid)
        def _():
            across(c).start()

        @pl.when(jnp.logical_not(is_mid))
        def _():
            to_mid(c).start()

    def spread(c):
        @pl.when(is_mid)
        def _():
            across(c).wait_recv()
            field[rows(blk), cols(c)] = (mid[c].astype(f32) + inner_in[c].astype(f32)).astype(bf16)

        @pl.when(jnp.logical_not(is_mid))
        def _():
            back(c).wait_recv()

        @pl.when(has_outer)
        def _():
            back(c).start()

        gather.own(c)

    by_walk = lambda c: c % every == 1
    relays = len([c for c in range(chunks) if c % every == 1]) if every else 0

    def first(c):
        gather.first(c, is_mid | jnp.logical_not(by_walk(c)) if every else c >= 0)

    def second(c):
        def relayed(block):
            @pl.when(is_mid & by_walk(c))
            def _():
                gather.copy(block, c, {"walk": outward}, fld_r).start()

        gather.second(c, relayed if every else None)

    def when_chunk(c, action):
        @pl.when((c >= 0) & (c < chunks))
        def _():
            action(c)

    def first_term(c):
        for e in range(2):
            for d in range(nb // 2):
                gather.landed((sibling + 2 * d) % nb, c - 1 + e)
        span = pl.ds(pl.multiple_of((c - 1) * size, 2 * size), 2 * size)
        terms[0, :, span] = jnp.dot(flat[...], field[:, span], preferred_element_type=f32).astype(bf16)

    def bias(b):
        wide[...] = widen([thetas[b, w] for w in range(wdev)])

        @pl.loop(0, nb)
        def _(v):
            for w in range(wdev):
                sums[w, pl.ds(pl.multiple_of(v * 8, 8), 8)] = fold(vectors[v] * wide[:, w * 128:(w + 1) * 128])

        for w in range(wdev):
            fb_out[b, w:w + 1] = line_of(sums[w])

    bias_start = jnp.where(is_mid, 6, outer_lag - 1)
    bias_pace = jnp.where(is_mid, 2 if nb <= 8 else 1, 4 * chunks)

    @pl.loop(0, chunks + outer_lag + 8)
    def _(t):
        when_chunk(t - lag, spread)
        when_chunk(t, reduce_in)
        when_chunk(t - lag - 3, first)
        when_chunk(t - lag - 6, second)
        pl.when(t == bias_start)(thetas_arrive)
        begin = (t - bias_start) // bias_pace

        @pl.when((t >= bias_start) & ((t - bias_start) % bias_pace == 0) & (begin < nb))
        def _():
            @pl.loop(jnp.where(is_mid, begin, 0), jnp.where(is_mid, begin + 1, nb))
            def _(b):
                bias(b)

        @pl.when(((t - lag - 7) % 2 == 1) & (t - lag - 7 > 0) & (t - lag - 7 < chunks))
        def _():
            first_term(t - lag - 7)

    fb_in[pl.ds(blk, 1)] = fb_out[pl.ds(blk, 1)]
    biases_arrive = share(fb_in, lambda b: fb_out.at[b], blk, blk_peers, 3)

    width = orbitals // 2
    for order in range(2, orders):
        @pl.loop(0, orbitals // width)
        def _(n):
            span = pl.ds(pl.multiple_of(n * width, width), width)
            term = (jnp.dot(terms[order - 2], field[:, span], preferred_element_type=f32) / order).astype(bf16)
            if order == orders - 1:
                value = flat[:, span].astype(f32)
                for k in range(orders - 2):
                    value = value + terms[k, :, span].astype(f32)
                partial[:, span] = value + term.astype(f32)
                last[:, span] = term
            else:
                terms[order - 1, :, span] = term

    biases_arrive()
    value = fb_in[0]
    for b in range(1, nb):
        value = value + fb_in[b]
    fb[...] = value[:, 0:group]

    def drain(piece, send):
        pltpu.make_async_remote_copy(src_ref=piece, dst_ref=piece, send_sem=send, recv_sem=fld_recv.at[0, 0],
                                     device_id={"blk": sibling}, device_id_type=MESH).wait_send()

    def many(count, send):
        if count:
            drain(field.at[pl.ds(0, count * block_rows)], send)

    many(gather.nf - 1, fld_f)
    many(gather.ns - 1, fld_s)
    many(nb // 2, fld_b)
    if every:
        @pl.when(is_mid)
        def _():
            many((gather.ns - 1) * (gather.nf - 1), fld_w)
            drain(field.at[pl.ds(0, block_rows), pl.ds(0, relays * size)], fld_r)

        @pl.when(jnp.logical_not(is_mid))
        def _():
            drain(field.at[pl.ds(0, block_rows), pl.ds(0, (chunks - relays) * size)], fld_w)
    else:
        many((gather.ns - 1) * (gather.nf - 1), fld_w)

    @pl.when(is_mid)
    def _():
        drain(mid, mid_send)

    @pl.when(jnp.logical_not(is_mid))
    def _():
        drain(mid, in_send)

    @pl.when(has_outer)
    def _():
        drain(field.at[pl.ds(0, block_rows)], out_send)


def closing(field, last, partial, fb, shift, out, fb_out, shift_out, held, sems):
    orbitals = field.shape[1]
    width = orbitals // 4
    small = [pltpu.make_async_copy(src, dst, sems.at[4 + k]) for k, (src, dst) in enumerate(((fb, fb_out), (shift, shift_out)))]
    for copy in small:
        copy.start()
    copies = []
    for n in range(4):
        span = pl.ds(n * width, width)
        term = (jnp.dot(last[...], field[:, span], preferred_element_type=f32) / orders).astype(bf16)
        held[:, span] = (partial[:, span] + term.astype(f32)).astype(bf16)
        copies.append(pltpu.make_async_copy(held.at[:, span], out.at[:, span], sems.at[n]))
        copies[-1].start()
    for copy in small + copies:
        copy.wait()


def local(nb, nw, walkers, inv_intersection, rotated_chol, full_chol, field_noise):
    wdev, double_rows, orbitals = walkers.shape
    occupied = double_rows // 2
    group = field_noise.shape[0]
    per = rotated_chol.shape[0]
    local_count, block_rows, _ = full_chol.shape
    chunks = 16
    size = orbitals // chunks
    parts = nb // nw
    assert nb == parts * nw and parts in (1, 2)
    tiles = orbitals // nb // 128
    every = 3 if nw == 4 and nb == 8 else 0
    flat = walkers.reshape(wdev * double_rows, orbitals)
    inv = inv_intersection.transpose(0, 2, 1, 3).reshape(wdev * double_rows, occupied)
    rot = rotated_chol.transpose(1, 0, 2).reshape(occupied, per, orbitals // 128, 128).transpose(0, 2, 1, 3)
    vmem, hbm = pl.BlockSpec(memory_space=pltpu.VMEM), pl.BlockSpec(memory_space=pltpu.HBM)
    dma = pltpu.SemaphoreType.DMA
    span = orbitals // parts
    results = pl.pallas_call(
        functools.partial(kernel, nb, nw, wdev * nb * nw, chunks, parts, every),
        out_shape=(pltpu.VMEM((orbitals, orbitals), bf16), pltpu.VMEM(flat.shape, bf16), pltpu.VMEM(flat.shape, f32),
                   pltpu.VMEM((wdev, group), f32), pltpu.VMEM((1, group), f32)),
        in_specs=[hbm] * 6,
        out_specs=(vmem,) * 5,
        scratch_shapes=[
            pltpu.VMEM(flat.shape, bf16),
            pltpu.VMEM(walkers.shape, bf16),
            pltpu.VMEM(inv.shape, bf16),
            pltpu.VMEM((wdev, occupied, double_rows), bf16),
            pltpu.VMEM((1, group), f32),
            pltpu.VMEM(rot.shape, bf16),
            pltpu.VMEM((nb, occupied, tiles, per, 128), bf16),
            pltpu.VMEM(full_chol.shape, bf16),
            pltpu.VMEM((wdev, occupied, orbitals), bf16),
            pltpu.VMEM((nb, wdev, occupied, tiles * 128), bf16),
            pltpu.VMEM((2, occupied, span), f32),
            pltpu.VMEM((occupied, span), f32),
            pltpu.VMEM((nw, occupied, tiles * 128), bf16),
            pltpu.VMEM((nw, occupied, tiles * 128), bf16),
            pltpu.VMEM((nb, occupied * tiles * per, 128), f32),
            pltpu.VMEM((tiles, occupied * tiles * per, occupied), bf16),
            pltpu.VMEM((occupied * tiles * per, wdev * 128), f32),
            pltpu.VMEM((wdev, nb * 8, 128), f32),
            pltpu.VMEM((nb, wdev, 128), f32),
            pltpu.VMEM((nb, wdev, 128), f32),
            pltpu.VMEM((chunks, block_rows, size), bf16),
            pltpu.VMEM((chunks, block_rows, size), bf16),
            pltpu.VMEM((chunks, block_rows, size), bf16),
            pltpu.VMEM((nw, 1, 128), f32),
            pltpu.VMEM((nb, 1, 128), f32),
            pltpu.VMEM((orders - 2,) + flat.shape, bf16),
            dma((nb, chunks)), dma, dma, dma, dma, dma,
            dma((6,)), dma((7,)), dma((7,)),
            dma, dma((chunks,)), dma, dma((chunks,)), dma, dma((chunks,)),
        ],
        compiler_params=pltpu.CompilerParams(collective_id=0, has_side_effects=True, vmem_limit_bytes=38 * 2**20),
    )(*[pltpu.with_memory_space_constraint(each, pltpu.HBM)
        for each in (flat, walkers, inv, rot, full_chol, field_noise.reshape(1, group))])
    results = [pltpu.with_memory_space_constraint(result, pltpu.VMEM) for result in results]
    out, fb, shift = pl.pallas_call(
        closing,
        out_shape=(jax.ShapeDtypeStruct(flat.shape, bf16), jax.ShapeDtypeStruct((wdev, group), f32),
                   jax.ShapeDtypeStruct((1, group), f32)),
        in_specs=[vmem] * 5,
        out_specs=(hbm,) * 3,
        scratch_shapes=[pltpu.VMEM(flat.shape, bf16), dma((6,))],
        compiler_params=pltpu.CompilerParams(vmem_limit_bytes=16 * 2**20),
    )(*results)
    return (out.reshape(walkers.shape), fb, shift.reshape(group))


def solution(mesh):
    placed = (
        P(("blk", "walk"), None, None),
        P(("blk", "walk"), None, None, None),
        P("blk", None, None),
        P("walk", "blk", None),
        P(),
    )
    return jax.shard_map(
        functools.partial(local, mesh.shape["blk"], mesh.shape["walk"]),
        mesh=mesh,
        in_specs=placed,
        out_specs=(P(("blk", "walk"), None, None), P(("blk", "walk"), None), P()),
        check_vma=False,
    )
```

```python
import functools
import math

import jax
import jax.numpy as jnp
from jax import lax
from jax.experimental import pallas as pl
from jax.experimental.pallas import tpu as pltpu
from jax.sharding import PartitionSpec as P

time_root = 0.1
orders = 4
f32, bf16 = jnp.float32, jnp.bfloat16
MESH = pl.DeviceIdType.MESH


class Gather:
    def __init__(self, nb, ref_at, recv, send_f, send_s, send_w, send_b):
        self.nb, self.ref_at, self.recv = nb, ref_at, recv
        self.send_f, self.send_s, self.send_w, self.send_b = send_f, send_s, send_w, send_b
        me = lax.axis_index("blk")
        self.me, self.core = me, me % 2
        self.cols = 2 if nb % 4 == 0 else 1
        self.rows = nb // 2 // self.cols
        chip = me // 2
        col, row = chip % self.cols, chip // self.cols
        self.turn = self.core if self.rows == self.cols else 0
        self.f = (1 - self.turn) * col + self.turn * row
        self.s = (1 - self.turn) * row + self.turn * col
        self.nf, self.ns = self.cols, self.rows
        self.sibling = chip * 2 + 1 - self.core

    def at(self, i, j):
        f, s = (self.f + i) % self.nf, (self.s + j) % self.ns
        chip = (1 - self.turn) * (s * self.cols + f) + self.turn * (f * self.cols + s)
        return chip * 2 + self.core

    def copy(self, block, chunk, target, send):
        piece = self.ref_at(block, chunk)
        return pltpu.make_async_remote_copy(
            src_ref=piece, dst_ref=piece, send_sem=send, recv_sem=self.recv.at[block, chunk],
            device_id=target if isinstance(target, dict) else {"blk": target}, device_id_type=MESH)

    def landed(self, block, chunk):
        self.copy(block, chunk, self.sibling, self.send_b).wait_recv()

    def own(self, chunk):
        for i in range(1, self.nf):
            self.copy(self.me, chunk, self.at(i, 0), self.send_f).start()
        for j in range(1, self.ns):
            self.copy(self.me, chunk, self.at(0, j), self.send_s).start()
        self.copy(self.me, chunk, self.sibling, self.send_b).start()

    def first(self, chunk, forward):
        for i in range(1, self.nf):
            block = self.at(i, 0)
            self.landed(block, chunk)

            @pl.when(forward)
            def _():
                for j in range(1, self.ns):
                    self.copy(block, chunk, self.at(0, j), self.send_w).start()

            self.copy(block, chunk, self.sibling, self.send_b).start()

    def second(self, chunk, relayed):
        for j in range(1, self.ns):
            for i in range(self.nf):
                block = self.at(i, j)
                self.landed(block, chunk)
                if i and relayed is not None:
                    relayed(block)
                self.copy(block, chunk, self.sibling, self.send_b).start()


def kernel(nb, nw, total_walkers, chunks, parts, every, flat_hbm, three_hbm, inv_hbm, rot_hbm, full_hbm, noise_hbm,
           field, last, partial, fb, shift,
           flat, three, inv_raw, inv, noise, own_rot, rots, full, theta, thetas, pair, mine, zout, zin,
           vectors, spread_rows, wide, sums, fb_out, fb_in, mid, outer_in, inner_in, slots_w, slots_b, terms,
           fld_recv, fld_f, fld_s, fld_w, fld_b, fld_r,
           load, slot_send, slot_recv, in_send, in_recv, mid_send, mid_recv, out_send, out_recv):
    blk, walk = lax.axis_index("blk"), lax.axis_index("walk")
    wdev, occupied, orbitals = theta.shape
    per, tiles = rots.shape[3], rots.shape[2]
    group = nb * per
    slab = tiles * 128
    local_count, block_rows = full.shape[0], full.shape[1]
    size = orbitals // chunks

    loads = [pltpu.make_async_copy(src, dst, load.at[k]) for k, (src, dst) in enumerate((
        (inv_hbm, inv_raw), (three_hbm, three), (rot_hbm, own_rot), (noise_hbm, noise), (flat_hbm, flat), (full_hbm, full)))]
    for one in loads:
        one.start()
    load_inv, load_three, load_rot, load_noise, load_flat, load_full = loads
    barrier = pltpu.get_barrier_semaphore()
    for d in range(1, nb):
        pl.semaphore_signal(barrier, inc=1, device_id={"blk": (blk + d) % nb}, device_id_type=MESH)
    for d in range(1, nw):
        pl.semaphore_signal(barrier, inc=1, device_id={"walk": (walk + d) % nw}, device_id_type=MESH)

    def one_hot(shape, wanted):
        row, column = lax.broadcasted_iota(jnp.int32, shape, 0), lax.broadcasted_iota(jnp.int32, shape, 1)
        return jnp.where(wanted(row, column), 1.0, 0.0).astype(bf16)

    load_inv.wait()
    for w in range(wdev):
        whole = jnp.zeros((occupied, 2 * occupied), f32)
        for s in range(2):
            take = one_hot((occupied, inv_raw.shape[0]), lambda r, c: c == 2 * (r + w * occupied) + s)
            place = one_hot((occupied, 2 * occupied), lambda r, c: c == r + s * occupied)
            block = jnp.dot(take, inv_raw[...], preferred_element_type=f32).astype(bf16)
            whole = whole + jnp.dot(block, place, preferred_element_type=f32)
        inv[w] = whole.astype(bf16)
    for t in range(tiles):
        spread_rows[t] = one_hot(spread_rows.shape[1:],
                                 lambda r, c: (r >= (c * tiles + t) * per) & (r < (c * tiles + t + 1) * per))

    load_three.wait()
    load_rot.wait()
    pl.semaphore_wait(barrier, nb + nw - 2)

    def slab_of(b, z):
        return (b % 2) * nw + (b // 2 + z) % nw if parts == 2 else (b + z) % nw

    slab_columns = lambda s: pl.ds(pl.multiple_of(s * slab, slab), slab)
    home = slab_of(blk, walk)
    sibling = blk // 2 * 2 + 1 - blk % 2
    walk_peers = [({"walk": (walk + d) % nw}, (walk + d) % nw) for d in range(1, nw)]
    blk_peers = [({"blk": (blk + d) % nb}, (blk + d) % nb) for d in range(1, nb)]

    def share(slots, source_at, me, peers, k):
        for peer, slot in peers:
            pltpu.make_async_remote_copy(
                src_ref=source_at(slot), dst_ref=slots.at[me],
                send_sem=slot_send.at[k], recv_sem=slot_recv.at[k], device_id=peer, device_id_type=MESH).start()

        def finish():
            rest = slots.at[pl.ds(0, len(peers))]
            pltpu.make_async_remote_copy(
                src_ref=rest, dst_ref=rest, send_sem=slot_send.at[k], recv_sem=slot_recv.at[k],
                device_id=peers[0][0], device_id_type=MESH).wait()

        return finish

    rot_slab = lambda b: own_rot.at[:, pl.ds(slab_of(b, walk) * tiles, tiles)]
    rots_arrive = share(rots, rot_slab, blk, blk_peers, 0)
    keep_rot = pltpu.make_async_copy(rot_slab(blk), rots.at[blk], load.at[2])
    keep_rot.start()

    tile = 512
    span_width = mine.shape[1]

    def project(begin, into):
        for lo in range(0, span_width, tile):
            span = pl.ds(pl.multiple_of(begin + lo, tile), tile)
            both = jnp.zeros((occupied, tile), f32)
            for w in range(wdev):
                one = jnp.dot(inv[w], three[w, :, span], preferred_element_type=f32).astype(bf16)
                theta[w, :, span] = one
                both = both + one.astype(f32)
            into[:, lo:lo + tile] = both

    if parts == 2:
        project((1 - blk % 2) * span_width, pair.at[0])
        swap = pltpu.make_async_remote_copy(
            src_ref=pair.at[0], dst_ref=pair.at[1], send_sem=slot_send.at[4], recv_sem=slot_recv.at[4],
            device_id={"blk": sibling}, device_id_type=MESH)
        swap.start()
        project(blk % 2 * span_width, mine)
        swap.wait()
    else:
        project(0, mine)
    for k in range(nw):
        columns = slab_columns(slab_of(blk, k) % nw)
        value = mine[:, columns]
        if parts == 2:
            value = value + pair[1, :, columns]
        zout[k] = value.astype(bf16)
    zin[pl.ds(walk, 1)] = zout[pl.ds(walk, 1)]
    sums_arrive = share(zin, lambda z: zout.at[z], walk, walk_peers, 1)
    def send_thetas(w):
        return share(thetas.at[w], lambda b: theta.at[w, :, slab_columns(slab_of(b, walk))], blk, blk_peers,
                     2 if w == 0 else 6 + w)

    early = (wdev + 1) // 2
    thetas_arrive = [send_thetas(w) for w in range(early)]
    for w in range(wdev):
        thetas[w, pl.ds(blk, 1)] = theta[pl.ds(w, 1), :, slab_columns(home)]

    def widen(narrow):
        pieces = []
        for t in range(tiles):
            side = [each[:, t * 128:(t + 1) * 128] for each in narrow]
            side = side[0] if len(side) == 1 else jnp.concatenate(side, axis=1)
            pieces.append(jnp.dot(spread_rows[t], side, preferred_element_type=f32))
        return functools.reduce(jnp.add, pieces)

    deep = spread_rows.shape[1]
    fold = lambda value: jnp.sum(value.reshape(deep // 8, 8, 128), axis=0)
    row = lax.broadcasted_iota(jnp.int32, (nb * 8, 128), 0)
    lane = lax.broadcasted_iota(jnp.int32, (nb * 8, 128), 1)
    picked = lane == row // 8 * per + row % per

    def line_of(value):
        return jnp.sum(jnp.where(picked, jnp.sum(value, axis=1, keepdims=True), 0.0), axis=0, keepdims=True)

    keep_rot.wait()
    rots_arrive()
    for b in range(nb):
        vectors[b] = rots.at[b].reshape(deep, 128)[...].astype(f32)
    sums_arrive()
    value = zin[0].astype(f32)
    for k in range(1, nw):
        value = value + zin[k].astype(f32)
    wide[:, 0:128] = widen([value.astype(bf16)])
    for b in range(nb):
        sums[0, b * 8:(b + 1) * 8] = fold(vectors[b] * wide[:, 0:128])
    line = line_of(sums[0])
    for peers, me, slots, k in ((walk_peers, walk, slots_w, 5), (blk_peers, blk, slots_b, 6)):
        slots[pl.ds(me, 1)] = line[None]
        share(slots, lambda slot: slots.at[me], me, peers, k)()
        line = slots[0]
        for d in range(1, slots.shape[0]):
            line = line + slots[d]
    thetas_arrive += [send_thetas(w) for w in range(early, wdev)]
    shifts = line / math.sqrt(total_walkers)
    shift[...] = shifts[:, 0:group]
    load_noise.wait()
    shifted = (noise[...] - shifts[:, 0:group]) * time_root
    lanes = lax.broadcasted_iota(jnp.int32, (1, group), 1)
    weights = [jnp.sum(jnp.where(lanes == walk * local_count + j, shifted, 0.0), axis=1, keepdims=True)
               for j in range(local_count)]
    load_full.wait()
    load_flat.wait()

    half = nw // 2
    is_mid = (walk == half - 1) | (walk == half)
    has_outer = (walk != 0) & (walk != nw - 1)
    step = 1 - 2 * (walk >= half).astype(jnp.int32)
    inward = (walk + step + nw) % nw
    outward = (walk - step + nw) % nw
    outer_lag = min(12, chunks)
    lag = jnp.where(is_mid, 3, outer_lag)
    cols = lambda c: pl.ds(pl.multiple_of(c * size, size), size)
    rows = lambda block: pl.ds(pl.multiple_of(block * block_rows, block_rows), block_rows)
    part_at = lambda block, c: field.at[rows(block), cols(c)]
    gather = Gather(nb, part_at, fld_recv, fld_f, fld_s, fld_w, fld_b)

    def hop(src, dst, send, recv, target):
        return pltpu.make_async_remote_copy(src_ref=src, dst_ref=dst, send_sem=send, recv_sem=recv,
                                            device_id={"walk": target}, device_id_type=MESH)

    def to_mid(c):
        return hop(mid.at[c], outer_in.at[c], in_send, in_recv.at[c], inward)

    def across(c):
        return hop(mid.at[c], inner_in.at[c], mid_send, mid_recv.at[c], inward)

    def back(c):
        return hop(part_at(blk, c), part_at(blk, c), out_send, out_recv.at[c], outward)

    def reduce_in(c):
        value = weights[0] * full[0, :, cols(c)].astype(f32)
        for j in range(1, local_count):
            value = value + weights[j] * full[j, :, cols(c)].astype(f32)

        @pl.when(has_outer)
        def _():
            to_mid(c).wait_recv()
            mid[c] = (value + outer_in[c].astype(f32)).astype(bf16)

        @pl.when(jnp.logical_not(has_outer))
        def _():
            mid[c] = value.astype(bf16)

        @pl.when(is_mid)
        def _():
            across(c).start()

        @pl.when(jnp.logical_not(is_mid))
        def _():
            to_mid(c).start()

    def spread(c):
        @pl.when(is_mid)
        def _():
            across(c).wait_recv()
            field[rows(blk), cols(c)] = (mid[c].astype(f32) + inner_in[c].astype(f32)).astype(bf16)

        @pl.when(jnp.logical_not(is_mid))
        def _():
            back(c).wait_recv()

        @pl.when(has_outer)
        def _():
            back(c).start()

        gather.own(c)

    by_walk = lambda c: c % every == 1
    relays = len([c for c in range(chunks) if c % every == 1]) if every else 0

    def first(c):
        gather.first(c, is_mid | jnp.logical_not(by_walk(c)) if every else c >= 0)

    def second(c):
        def relayed(block):
            @pl.when(is_mid & by_walk(c))
            def _():
                gather.copy(block, c, {"walk": outward}, fld_r).start()

        gather.second(c, relayed if every else None)

    def when_chunk(c, action):
        @pl.when((c >= 0) & (c < chunks))
        def _():
            action(c)

    def first_term(c):
        for e in range(2):
            for d in range(nb // 2):
                gather.landed((sibling + 2 * d) % nb, c - 1 + e)
        span = pl.ds(pl.multiple_of((c - 1) * size, 2 * size), 2 * size)
        terms[0, :, span] = jnp.dot(flat[...], field[:, span], preferred_element_type=f32).astype(bf16)

    def bias(b):
        wide[...] = widen([thetas[w, b] for w in range(wdev)])

        @pl.loop(0, nb)
        def _(v):
            for w in range(wdev):
                sums[w, pl.ds(pl.multiple_of(v * 8, 8), 8)] = fold(vectors[v] * wide[:, w * 128:(w + 1) * 128])

        for w in range(wdev):
            fb_out[b, w:w + 1] = line_of(sums[w])

    split = orbitals * 3 // 4
    ready = split // size - 1
    bias_start = jnp.where(is_mid, 6, outer_lag - 1)
    bias_pace = jnp.where(is_mid, 2 if nb <= 8 else 1, 4 * chunks)

    @pl.loop(0, chunks + outer_lag + 8)
    def _(t):
        when_chunk(t - lag, spread)
        when_chunk(t, reduce_in)
        when_chunk(t - lag - 3, first)
        when_chunk(t - lag - 6, second)
        @pl.when(t == bias_start)
        def _():
            for arrive in thetas_arrive:
                arrive()

        begin = (t - bias_start) // bias_pace

        @pl.when((t >= bias_start) & ((t - bias_start) % bias_pace == 0) & (begin < nb))
        def _():
            @pl.loop(jnp.where(is_mid, begin, 0), jnp.where(is_mid, begin + 1, nb))
            def _(b):
                bias(b)

        @pl.when(((t - lag - 7) % 2 == 1) & (t - lag - 7 > 0) & (t - lag - 7 < chunks))
        def _():
            first_term(t - lag - 7)

        piece = t - lag - 7 - ready

        @pl.when((piece >= 0) & (piece < split // tile))
        def _():
            span = pl.ds(pl.multiple_of(piece * tile, tile), tile)
            partial[:, span] = jnp.dot(terms[0, :, 0:split], field[0:split, span], preferred_element_type=f32)

    fb_in[pl.ds(blk, 1)] = fb_out[pl.ds(blk, 1)]
    biases_arrive = share(fb_in, lambda b: fb_out.at[b], blk, blk_peers, 3)

    for n in range(orbitals // tile):
        span = slice(n * tile, (n + 1) * tile)
        if n < split // tile:
            value = partial[:, span] + jnp.dot(terms[0, :, split:], field[split:, span], preferred_element_type=f32)
        else:
            value = jnp.dot(terms[0], field[:, span], preferred_element_type=f32)
        terms[1, :, span] = (value / 2).astype(bf16)

    width = orbitals // 2
    for order in range(3, orders):
        @pl.loop(0, orbitals // width)
        def _(n):
            span = pl.ds(pl.multiple_of(n * width, width), width)
            term = (jnp.dot(terms[order - 2], field[:, span], preferred_element_type=f32) / order).astype(bf16)
            if order == orders - 1:
                value = flat[:, span].astype(f32)
                for k in range(orders - 2):
                    value = value + terms[k, :, span].astype(f32)
                partial[:, span] = value + term.astype(f32)
                last[:, span] = term
            else:
                terms[order - 1, :, span] = term

    biases_arrive()
    value = fb_in[0]
    for b in range(1, nb):
        value = value + fb_in[b]
    fb[...] = value[:, 0:group]

    def drain(piece, send):
        pltpu.make_async_remote_copy(src_ref=piece, dst_ref=piece, send_sem=send, recv_sem=fld_recv.at[0, 0],
                                     device_id={"blk": sibling}, device_id_type=MESH).wait_send()

    def many(count, send):
        if count:
            drain(field.at[pl.ds(0, count * block_rows)], send)

    many(gather.nf - 1, fld_f)
    many(gather.ns - 1, fld_s)
    many(nb // 2, fld_b)
    if every:
        @pl.when(is_mid)
        def _():
            many((gather.ns - 1) * (gather.nf - 1), fld_w)
            drain(field.at[pl.ds(0, block_rows), pl.ds(0, relays * size)], fld_r)

        @pl.when(jnp.logical_not(is_mid))
        def _():
            drain(field.at[pl.ds(0, block_rows), pl.ds(0, (chunks - relays) * size)], fld_w)
    else:
        many((gather.ns - 1) * (gather.nf - 1), fld_w)

    @pl.when(is_mid)
    def _():
        drain(mid, mid_send)

    @pl.when(jnp.logical_not(is_mid))
    def _():
        drain(mid, in_send)

    @pl.when(has_outer)
    def _():
        drain(field.at[pl.ds(0, block_rows)], out_send)


def closing(field, last, partial, fb, shift, out, fb_out, shift_out, held, sems):
    orbitals = field.shape[1]
    width = orbitals // 8
    small = [pltpu.make_async_copy(src, dst, sems.at[8 + k]) for k, (src, dst) in enumerate(((fb, fb_out), (shift, shift_out)))]
    for copy in small:
        copy.start()
    copies = []
    for n in range(8):
        span = pl.ds(n * width, width)
        term = (jnp.dot(last[...], field[:, span], preferred_element_type=f32) / orders).astype(bf16)
        held[:, span] = (partial[:, span] + term.astype(f32)).astype(bf16)
        copies.append(pltpu.make_async_copy(held.at[:, span], out.at[:, span], sems.at[n]))
        copies[-1].start()
    for copy in small + copies:
        copy.wait()


def local(nb, nw, walkers, inv_intersection, rotated_chol, full_chol, field_noise):
    wdev, double_rows, orbitals = walkers.shape
    occupied = double_rows // 2
    group = field_noise.shape[0]
    per = rotated_chol.shape[0]
    local_count, block_rows, _ = full_chol.shape
    chunks = 16
    size = orbitals // chunks
    parts = nb // nw
    assert nb == parts * nw and parts in (1, 2)
    tiles = orbitals // nb // 128
    every = 3 if nw == 4 and nb == 8 else 0
    flat = walkers.reshape(wdev * double_rows, orbitals)
    inv = inv_intersection.transpose(0, 2, 1, 3).reshape(wdev * double_rows, occupied)
    rot = rotated_chol.transpose(1, 0, 2).reshape(occupied, per, orbitals // 128, 128).transpose(0, 2, 1, 3)
    vmem, hbm = pl.BlockSpec(memory_space=pltpu.VMEM), pl.BlockSpec(memory_space=pltpu.HBM)
    dma = pltpu.SemaphoreType.DMA
    span = orbitals // parts
    results = pl.pallas_call(
        functools.partial(kernel, nb, nw, wdev * nb * nw, chunks, parts, every),
        out_shape=(pltpu.VMEM((orbitals, orbitals), bf16), pltpu.VMEM(flat.shape, bf16), pltpu.VMEM(flat.shape, f32),
                   pltpu.VMEM((wdev, group), f32), pltpu.VMEM((1, group), f32)),
        in_specs=[hbm] * 6,
        out_specs=(vmem,) * 5,
        scratch_shapes=[
            pltpu.VMEM(flat.shape, bf16),
            pltpu.VMEM(walkers.shape, bf16),
            pltpu.VMEM(inv.shape, bf16),
            pltpu.VMEM((wdev, occupied, double_rows), bf16),
            pltpu.VMEM((1, group), f32),
            pltpu.VMEM(rot.shape, bf16),
            pltpu.VMEM((nb, occupied, tiles, per, 128), bf16),
            pltpu.VMEM(full_chol.shape, bf16),
            pltpu.VMEM((wdev, occupied, orbitals), bf16),
            pltpu.VMEM((wdev, nb, occupied, tiles * 128), bf16),
            pltpu.VMEM((2, occupied, span), f32),
            pltpu.VMEM((occupied, span), f32),
            pltpu.VMEM((nw, occupied, tiles * 128), bf16),
            pltpu.VMEM((nw, occupied, tiles * 128), bf16),
            pltpu.VMEM((nb, occupied * tiles * per, 128), f32),
            pltpu.VMEM((tiles, occupied * tiles * per, occupied), bf16),
            pltpu.VMEM((occupied * tiles * per, wdev * 128), f32),
            pltpu.VMEM((wdev, nb * 8, 128), f32),
            pltpu.VMEM((nb, wdev, 128), f32),
            pltpu.VMEM((nb, wdev, 128), f32),
            pltpu.VMEM((chunks, block_rows, size), bf16),
            pltpu.VMEM((chunks, block_rows, size), bf16),
            pltpu.VMEM((chunks, block_rows, size), bf16),
            pltpu.VMEM((nw, 1, 128), f32),
            pltpu.VMEM((nb, 1, 128), f32),
            pltpu.VMEM((orders - 2,) + flat.shape, bf16),
            dma((nb, chunks)), dma, dma, dma, dma, dma,
            dma((6,)), dma((7 + wdev,)), dma((7 + wdev,)),
            dma, dma((chunks,)), dma, dma((chunks,)), dma, dma((chunks,)),
        ],
        compiler_params=pltpu.CompilerParams(collective_id=0, has_side_effects=True, vmem_limit_bytes=38 * 2**20),
    )(*[pltpu.with_memory_space_constraint(each, pltpu.HBM)
        for each in (flat, walkers, inv, rot, full_chol, field_noise.reshape(1, group))])
    results = [pltpu.with_memory_space_constraint(result, pltpu.VMEM) for result in results]
    out, fb, shift = pl.pallas_call(
        closing,
        out_shape=(jax.ShapeDtypeStruct(flat.shape, bf16), jax.ShapeDtypeStruct((wdev, group), f32),
                   jax.ShapeDtypeStruct((1, group), f32)),
        in_specs=[vmem] * 5,
        out_specs=(hbm,) * 3,
        scratch_shapes=[pltpu.VMEM(flat.shape, bf16), dma((10,))],
        compiler_params=pltpu.CompilerParams(vmem_limit_bytes=16 * 2**20),
    )(*results)
    return (out.reshape(walkers.shape), fb, shift.reshape(group))


def solution(mesh):
    placed = (
        P(("blk", "walk"), None, None),
        P(("blk", "walk"), None, None, None),
        P("blk", None, None),
        P("walk", "blk", None),
        P(),
    )
    return jax.shard_map(
        functools.partial(local, mesh.shape["blk"], mesh.shape["walk"]),
        mesh=mesh,
        in_specs=placed,
        out_specs=(P(("blk", "walk"), None, None), P(("blk", "walk"), None), P()),
        check_vma=False,
    )
```

```python
import functools
import math

import jax
import jax.numpy as jnp
from jax import lax
from jax.experimental import pallas as pl
from jax.experimental.pallas import tpu as pltpu
from jax.sharding import PartitionSpec as P

time_root = 0.1
orders = 4
f32, bf16 = jnp.float32, jnp.bfloat16
MESH = pl.DeviceIdType.MESH


class Gather:
    def __init__(self, nb, ref_at, recv, send_f, send_s, send_w, send_b):
        self.nb, self.ref_at, self.recv = nb, ref_at, recv
        self.send_f, self.send_s, self.send_w, self.send_b = send_f, send_s, send_w, send_b
        me = lax.axis_index("blk")
        self.me, self.core = me, me % 2
        self.cols = 2 if nb % 4 == 0 else 1
        self.rows = nb // 2 // self.cols
        chip = me // 2
        col, row = chip % self.cols, chip // self.cols
        self.turn = self.core if self.rows == self.cols else 0
        self.f = (1 - self.turn) * col + self.turn * row
        self.s = (1 - self.turn) * row + self.turn * col
        self.nf, self.ns = self.cols, self.rows
        self.sibling = chip * 2 + 1 - self.core

    def at(self, i, j):
        f, s = (self.f + i) % self.nf, (self.s + j) % self.ns
        chip = (1 - self.turn) * (s * self.cols + f) + self.turn * (f * self.cols + s)
        return chip * 2 + self.core

    def copy(self, block, chunk, target, send):
        piece = self.ref_at(block, chunk)
        return pltpu.make_async_remote_copy(
            src_ref=piece, dst_ref=piece, send_sem=send, recv_sem=self.recv.at[block, chunk],
            device_id=target if isinstance(target, dict) else {"blk": target}, device_id_type=MESH)

    def landed(self, block, chunk):
        self.copy(block, chunk, self.sibling, self.send_b).wait_recv()

    def own(self, chunk):
        for i in range(1, self.nf):
            self.copy(self.me, chunk, self.at(i, 0), self.send_f).start()
        for j in range(1, self.ns):
            self.copy(self.me, chunk, self.at(0, j), self.send_s).start()
        self.copy(self.me, chunk, self.sibling, self.send_b).start()

    def first(self, chunk, forward):
        for i in range(1, self.nf):
            block = self.at(i, 0)
            self.landed(block, chunk)

            @pl.when(forward)
            def _():
                for j in range(1, self.ns):
                    self.copy(block, chunk, self.at(0, j), self.send_w).start()

            self.copy(block, chunk, self.sibling, self.send_b).start()

    def second(self, chunk, relayed):
        for j in range(1, self.ns):
            for i in range(self.nf):
                block = self.at(i, j)
                self.landed(block, chunk)
                if i and relayed is not None:
                    relayed(block)
                self.copy(block, chunk, self.sibling, self.send_b).start()


def kernel(nb, nw, total_walkers, chunks, parts, every, flat_hbm, three_hbm, inv_hbm, rot_hbm, full_hbm, noise_hbm,
           field, last, partial, fb, shift,
           flat, three, inv_raw, inv, noise, own_rot, rots, full, theta, thetas, pair, mine, zout, zin,
           vectors, spread_rows, wide, sums, fb_out, fb_in, mid, outer_in, inner_in, slots_w, slots_b, terms,
           fld_recv, fld_f, fld_s, fld_w, fld_b, fld_r,
           load, slot_send, slot_recv, in_send, in_recv, mid_send, mid_recv, out_send, out_recv):
    blk, walk = lax.axis_index("blk"), lax.axis_index("walk")
    wdev, occupied, orbitals = theta.shape
    per, tiles = rots.shape[3], rots.shape[2]
    group = nb * per
    slab = tiles * 128
    local_count, block_rows = full.shape[0], full.shape[1]
    size = orbitals // chunks

    loads = [pltpu.make_async_copy(src, dst, load.at[k]) for k, (src, dst) in enumerate((
        (inv_hbm, inv_raw), (three_hbm, three), (rot_hbm, own_rot), (noise_hbm, noise), (flat_hbm, flat), (full_hbm, full)))]
    for one in loads[:4]:
        one.start()
    load_inv, load_three, load_rot, load_noise, load_flat, load_full = loads
    barrier = pltpu.get_barrier_semaphore()
    for d in range(1, nb):
        pl.semaphore_signal(barrier, inc=1, device_id={"blk": (blk + d) % nb}, device_id_type=MESH)
    for d in range(1, nw):
        pl.semaphore_signal(barrier, inc=1, device_id={"walk": (walk + d) % nw}, device_id_type=MESH)

    def one_hot(shape, wanted):
        row, column = lax.broadcasted_iota(jnp.int32, shape, 0), lax.broadcasted_iota(jnp.int32, shape, 1)
        return jnp.where(wanted(row, column), 1.0, 0.0).astype(bf16)

    load_inv.wait()
    for w in range(wdev):
        whole = jnp.zeros((occupied, 2 * occupied), f32)
        for s in range(2):
            take = one_hot((occupied, inv_raw.shape[0]), lambda r, c: c == 2 * (r + w * occupied) + s)
            place = one_hot((occupied, 2 * occupied), lambda r, c: c == r + s * occupied)
            block = jnp.dot(take, inv_raw[...], preferred_element_type=f32).astype(bf16)
            whole = whole + jnp.dot(block, place, preferred_element_type=f32)
        inv[w] = whole.astype(bf16)
    for t in range(tiles):
        spread_rows[t] = one_hot(spread_rows.shape[1:],
                                 lambda r, c: (r >= (c * tiles + t) * per) & (r < (c * tiles + t + 1) * per))

    load_three.wait()
    load_rot.wait()
    for one in loads[4:]:
        one.start()
    pl.semaphore_wait(barrier, nb + nw - 2)

    def slab_of(b, z):
        return (b % 2) * nw + (b // 2 + z) % nw if parts == 2 else (b + z) % nw

    slab_columns = lambda s: pl.ds(pl.multiple_of(s * slab, slab), slab)
    home = slab_of(blk, walk)
    sibling = blk // 2 * 2 + 1 - blk % 2
    walk_peers = [({"walk": (walk + d) % nw}, (walk + d) % nw) for d in range(1, nw)]
    blk_peers = [({"blk": (blk + d) % nb}, (blk + d) % nb) for d in range(1, nb)]

    def share(slots, source_at, me, peers, k):
        for peer, slot in peers:
            pltpu.make_async_remote_copy(
                src_ref=source_at(slot), dst_ref=slots.at[me],
                send_sem=slot_send.at[k], recv_sem=slot_recv.at[k], device_id=peer, device_id_type=MESH).start()

        def finish():
            rest = slots.at[pl.ds(0, len(peers))]
            pltpu.make_async_remote_copy(
                src_ref=rest, dst_ref=rest, send_sem=slot_send.at[k], recv_sem=slot_recv.at[k],
                device_id=peers[0][0], device_id_type=MESH).wait()

        return finish

    rot_slab = lambda b: own_rot.at[:, pl.ds(slab_of(b, walk) * tiles, tiles)]
    rots_arrive = share(rots, rot_slab, blk, blk_peers, 0)
    keep_rot = pltpu.make_async_copy(rot_slab(blk), rots.at[blk], load.at[2])
    keep_rot.start()

    tile = 512
    span_width = mine.shape[1]

    def project(begin, into):
        for lo in range(0, span_width, tile):
            span = pl.ds(pl.multiple_of(begin + lo, tile), tile)
            both = jnp.zeros((occupied, tile), f32)
            for w in range(wdev):
                one = jnp.dot(inv[w], three[w, :, span], preferred_element_type=f32).astype(bf16)
                theta[w, :, span] = one
                both = both + one.astype(f32)
            into[:, lo:lo + tile] = both

    if parts == 2:
        project((1 - blk % 2) * span_width, pair.at[0])
        swap = pltpu.make_async_remote_copy(
            src_ref=pair.at[0], dst_ref=pair.at[1], send_sem=slot_send.at[4], recv_sem=slot_recv.at[4],
            device_id={"blk": sibling}, device_id_type=MESH)
        swap.start()
        project(blk % 2 * span_width, mine)
        swap.wait()
    else:
        project(0, mine)
    for k in range(nw):
        columns = slab_columns(slab_of(blk, k) % nw)
        value = mine[:, columns]
        if parts == 2:
            value = value + pair[1, :, columns]
        zout[k] = value.astype(bf16)
    zin[pl.ds(walk, 1)] = zout[pl.ds(walk, 1)]
    sums_arrive = share(zin, lambda z: zout.at[z], walk, walk_peers, 1)
    def send_thetas(w):
        return share(thetas.at[w], lambda b: theta.at[w, :, slab_columns(slab_of(b, walk))], blk, blk_peers,
                     2 if w == 0 else 6 + w)

    early = (wdev + 1) // 2
    thetas_arrive = [send_thetas(w) for w in range(early)]
    for w in range(wdev):
        thetas[w, pl.ds(blk, 1)] = theta[pl.ds(w, 1), :, slab_columns(home)]

    def widen(narrow):
        pieces = []
        for t in range(tiles):
            side = [each[:, t * 128:(t + 1) * 128] for each in narrow]
            side = side[0] if len(side) == 1 else jnp.concatenate(side, axis=1)
            pieces.append(jnp.dot(spread_rows[t], side, preferred_element_type=f32))
        return functools.reduce(jnp.add, pieces)

    deep = spread_rows.shape[1]
    fold = lambda value: jnp.sum(value.reshape(deep // 8, 8, 128), axis=0)
    row = lax.broadcasted_iota(jnp.int32, (nb * 8, 128), 0)
    lane = lax.broadcasted_iota(jnp.int32, (nb * 8, 128), 1)
    picked = lane == row // 8 * per + row % per

    def line_of(value):
        return jnp.sum(jnp.where(picked, jnp.sum(value, axis=1, keepdims=True), 0.0), axis=0, keepdims=True)

    keep_rot.wait()
    rots_arrive()
    for b in range(nb):
        vectors[b] = rots.at[b].reshape(deep, 128)[...].astype(f32)
    sums_arrive()
    value = zin[0].astype(f32)
    for k in range(1, nw):
        value = value + zin[k].astype(f32)
    wide[:, 0:128] = widen([value.astype(bf16)])
    for b in range(nb):
        sums[0, b * 8:(b + 1) * 8] = fold(vectors[b] * wide[:, 0:128])
    line = line_of(sums[0])
    for peers, me, slots, k in ((walk_peers, walk, slots_w, 5), (blk_peers, blk, slots_b, 6)):
        slots[pl.ds(me, 1)] = line[None]
        share(slots, lambda slot: slots.at[me], me, peers, k)()
        line = slots[0]
        for d in range(1, slots.shape[0]):
            line = line + slots[d]
    thetas_arrive += [send_thetas(w) for w in range(early, wdev)]
    shifts = line / math.sqrt(total_walkers)
    shift[...] = shifts[:, 0:group]
    load_noise.wait()
    shifted = (noise[...] - shifts[:, 0:group]) * time_root
    lanes = lax.broadcasted_iota(jnp.int32, (1, group), 1)
    weights = [jnp.sum(jnp.where(lanes == walk * local_count + j, shifted, 0.0), axis=1, keepdims=True)
               for j in range(local_count)]
    load_full.wait()
    load_flat.wait()

    half = nw // 2
    is_mid = (walk == half - 1) | (walk == half)
    has_outer = (walk != 0) & (walk != nw - 1)
    step = 1 - 2 * (walk >= half).astype(jnp.int32)
    inward = (walk + step + nw) % nw
    outward = (walk - step + nw) % nw
    outer_lag = min(12, chunks)
    lag = jnp.where(is_mid, 3, outer_lag)
    cols = lambda c: pl.ds(pl.multiple_of(c * size, size), size)
    rows = lambda block: pl.ds(pl.multiple_of(block * block_rows, block_rows), block_rows)
    part_at = lambda block, c: field.at[rows(block), cols(c)]
    gather = Gather(nb, part_at, fld_recv, fld_f, fld_s, fld_w, fld_b)

    def hop(src, dst, send, recv, target):
        return pltpu.make_async_remote_copy(src_ref=src, dst_ref=dst, send_sem=send, recv_sem=recv,
                                            device_id={"walk": target}, device_id_type=MESH)

    def to_mid(c):
        return hop(mid.at[c], outer_in.at[c], in_send, in_recv.at[c], inward)

    def across(c):
        return hop(mid.at[c], inner_in.at[c], mid_send, mid_recv.at[c], inward)

    def back(c):
        return hop(part_at(blk, c), part_at(blk, c), out_send, out_recv.at[c], outward)

    def reduce_in(c):
        value = weights[0] * full[0, :, cols(c)].astype(f32)
        for j in range(1, local_count):
            value = value + weights[j] * full[j, :, cols(c)].astype(f32)

        @pl.when(has_outer)
        def _():
            to_mid(c).wait_recv()
            mid[c] = (value + outer_in[c].astype(f32)).astype(bf16)

        @pl.when(jnp.logical_not(has_outer))
        def _():
            mid[c] = value.astype(bf16)

        @pl.when(is_mid)
        def _():
            across(c).start()

        @pl.when(jnp.logical_not(is_mid))
        def _():
            to_mid(c).start()

    def spread(c):
        @pl.when(is_mid)
        def _():
            across(c).wait_recv()
            field[rows(blk), cols(c)] = (mid[c].astype(f32) + inner_in[c].astype(f32)).astype(bf16)

        @pl.when(jnp.logical_not(is_mid))
        def _():
            back(c).wait_recv()

        @pl.when(has_outer)
        def _():
            back(c).start()

        gather.own(c)

    by_walk = lambda c: (c % 2 == 1) & (c < 10)
    relays = len([c for c in range(chunks) if c % 2 == 1 and c < 10]) if every else 0

    def first(c):
        gather.first(c, is_mid | jnp.logical_not(by_walk(c)) if every else c >= 0)

    def second(c):
        def relayed(block):
            @pl.when(is_mid & by_walk(c))
            def _():
                gather.copy(block, c, {"walk": outward}, fld_r).start()

        gather.second(c, relayed if every else None)

    def when_chunk(c, action):
        @pl.when((c >= 0) & (c < chunks))
        def _():
            action(c)

    def first_term(c):
        for e in range(2):
            for d in range(nb // 2):
                gather.landed((sibling + 2 * d) % nb, c - 1 + e)
        span = pl.ds(pl.multiple_of((c - 1) * size, 2 * size), 2 * size)
        terms[0, :, span] = jnp.dot(flat[...], field[:, span], preferred_element_type=f32).astype(bf16)

    def bias(b):
        wide[...] = widen([thetas[w, b] for w in range(wdev)])

        @pl.loop(0, nb)
        def _(v):
            for w in range(wdev):
                sums[w, pl.ds(pl.multiple_of(v * 8, 8), 8)] = fold(vectors[v] * wide[:, w * 128:(w + 1) * 128])

        for w in range(wdev):
            fb_out[b, w:w + 1] = line_of(sums[w])

    split = orbitals * 3 // 4
    ready = split // size - 1
    bias_start = jnp.where(is_mid, 6, outer_lag - 1)
    bias_pace = jnp.where(is_mid, 2 if nb <= 8 else 1, 4 * chunks)

    @pl.loop(0, chunks + outer_lag + 11)
    def _(t):
        when_chunk(t - lag, spread)
        when_chunk(t, reduce_in)
        when_chunk(t - lag - 3, first)
        when_chunk(t - lag - 9, second)
        @pl.when(t == bias_start)
        def _():
            for arrive in thetas_arrive:
                arrive()

        begin = (t - bias_start) // bias_pace

        @pl.when((t >= bias_start) & ((t - bias_start) % bias_pace == 0) & (begin < nb))
        def _():
            @pl.loop(jnp.where(is_mid, begin, 0), jnp.where(is_mid, begin + 1, nb))
            def _(b):
                bias(b)

        @pl.when(((t - lag - 10) % 2 == 1) & (t - lag - 10 > 0) & (t - lag - 10 < chunks))
        def _():
            first_term(t - lag - 10)

        piece = t - lag - 10 - ready

        @pl.when((piece >= 0) & (piece < split // tile))
        def _():
            span = pl.ds(pl.multiple_of(piece * tile, tile), tile)
            partial[:, span] = jnp.dot(terms[0, :, 0:split], field[0:split, span], preferred_element_type=f32)

    fb_in[pl.ds(blk, 1)] = fb_out[pl.ds(blk, 1)]
    biases_arrive = share(fb_in, lambda b: fb_out.at[b], blk, blk_peers, 3)

    for n in range(orbitals // tile):
        span = slice(n * tile, (n + 1) * tile)
        if n < split // tile:
            value = partial[:, span] + jnp.dot(terms[0, :, split:], field[split:, span], preferred_element_type=f32)
        else:
            value = jnp.dot(terms[0], field[:, span], preferred_element_type=f32)
        terms[1, :, span] = (value / 2).astype(bf16)

    width = orbitals // 2
    for order in range(3, orders):
        @pl.loop(0, orbitals // width)
        def _(n):
            span = pl.ds(pl.multiple_of(n * width, width), width)
            term = (jnp.dot(terms[order - 2], field[:, span], preferred_element_type=f32) / order).astype(bf16)
            if order == orders - 1:
                value = flat[:, span].astype(f32)
                for k in range(orders - 2):
                    value = value + terms[k, :, span].astype(f32)
                partial[:, span] = value + term.astype(f32)
                last[:, span] = term
            else:
                terms[order - 1, :, span] = term

    biases_arrive()
    value = fb_in[0]
    for b in range(1, nb):
        value = value + fb_in[b]
    fb[...] = value[:, 0:group]

    def drain(piece, send):
        pltpu.make_async_remote_copy(src_ref=piece, dst_ref=piece, send_sem=send, recv_sem=fld_recv.at[0, 0],
                                     device_id={"blk": sibling}, device_id_type=MESH).wait_send()

    def many(count, send):
        if count:
            drain(field.at[pl.ds(0, count * block_rows)], send)

    many(gather.nf - 1, fld_f)
    many(gather.ns - 1, fld_s)
    many(nb // 2, fld_b)
    if every:
        @pl.when(is_mid)
        def _():
            many((gather.ns - 1) * (gather.nf - 1), fld_w)
            drain(field.at[pl.ds(0, block_rows), pl.ds(0, relays * size)], fld_r)

        @pl.when(jnp.logical_not(is_mid))
        def _():
            drain(field.at[pl.ds(0, block_rows), pl.ds(0, (chunks - relays) * size)], fld_w)
    else:
        many((gather.ns - 1) * (gather.nf - 1), fld_w)

    @pl.when(is_mid)
    def _():
        drain(mid, mid_send)

    @pl.when(jnp.logical_not(is_mid))
    def _():
        drain(mid, in_send)

    @pl.when(has_outer)
    def _():
        drain(field.at[pl.ds(0, block_rows)], out_send)


def closing(field, last, partial, fb, shift, out, fb_out, shift_out, held, sems):
    orbitals = field.shape[1]
    width = orbitals // 8
    small = [pltpu.make_async_copy(src, dst, sems.at[8 + k]) for k, (src, dst) in enumerate(((fb, fb_out), (shift, shift_out)))]
    for copy in small:
        copy.start()
    copies = []
    for n in range(8):
        span = pl.ds(n * width, width)
        term = (jnp.dot(last[...], field[:, span], preferred_element_type=f32) / orders).astype(bf16)
        held[:, span] = (partial[:, span] + term.astype(f32)).astype(bf16)
        copies.append(pltpu.make_async_copy(held.at[:, span], out.at[:, span], sems.at[n]))
        copies[-1].start()
    for copy in small + copies:
        copy.wait()


def local(nb, nw, walkers, inv_intersection, rotated_chol, full_chol, field_noise):
    wdev, double_rows, orbitals = walkers.shape
    occupied = double_rows // 2
    group = field_noise.shape[0]
    per = rotated_chol.shape[0]
    local_count, block_rows, _ = full_chol.shape
    chunks = 16
    size = orbitals // chunks
    parts = nb // nw
    assert nb == parts * nw and parts in (1, 2)
    tiles = orbitals // nb // 128
    every = 3 if nw == 4 and nb == 8 else 0
    flat = walkers.reshape(wdev * double_rows, orbitals)
    inv = inv_intersection.transpose(0, 2, 1, 3).reshape(wdev * double_rows, occupied)
    rot = rotated_chol.transpose(1, 0, 2).reshape(occupied, per, orbitals // 128, 128).transpose(0, 2, 1, 3)
    vmem, hbm = pl.BlockSpec(memory_space=pltpu.VMEM), pl.BlockSpec(memory_space=pltpu.HBM)
    dma = pltpu.SemaphoreType.DMA
    span = orbitals // parts
    results = pl.pallas_call(
        functools.partial(kernel, nb, nw, wdev * nb * nw, chunks, parts, every),
        out_shape=(pltpu.VMEM((orbitals, orbitals), bf16), pltpu.VMEM(flat.shape, bf16), pltpu.VMEM(flat.shape, f32),
                   pltpu.VMEM((wdev, group), f32), pltpu.VMEM((1, group), f32)),
        in_specs=[hbm] * 6,
        out_specs=(vmem,) * 5,
        scratch_shapes=[
            pltpu.VMEM(flat.shape, bf16),
            pltpu.VMEM(walkers.shape, bf16),
            pltpu.VMEM(inv.shape, bf16),
            pltpu.VMEM((wdev, occupied, double_rows), bf16),
            pltpu.VMEM((1, group), f32),
            pltpu.VMEM(rot.shape, bf16),
            pltpu.VMEM((nb, occupied, tiles, per, 128), bf16),
            pltpu.VMEM(full_chol.shape, bf16),
            pltpu.VMEM((wdev, occupied, orbitals), bf16),
            pltpu.VMEM((wdev, nb, occupied, tiles * 128), bf16),
            pltpu.VMEM((2, occupied, span), f32),
            pltpu.VMEM((occupied, span), f32),
            pltpu.VMEM((nw, occupied, tiles * 128), bf16),
            pltpu.VMEM((nw, occupied, tiles * 128), bf16),
            pltpu.VMEM((nb, occupied * tiles * per, 128), f32),
            pltpu.VMEM((tiles, occupied * tiles * per, occupied), bf16),
            pltpu.VMEM((occupied * tiles * per, wdev * 128), f32),
            pltpu.VMEM((wdev, nb * 8, 128), f32),
            pltpu.VMEM((nb, wdev, 128), f32),
            pltpu.VMEM((nb, wdev, 128), f32),
            pltpu.VMEM((chunks, block_rows, size), bf16),
            pltpu.VMEM((chunks, block_rows, size), bf16),
            pltpu.VMEM((chunks, block_rows, size), bf16),
            pltpu.VMEM((nw, 1, 128), f32),
            pltpu.VMEM((nb, 1, 128), f32),
            pltpu.VMEM((orders - 2,) + flat.shape, bf16),
            dma((nb, chunks)), dma, dma, dma, dma, dma,
            dma((6,)), dma((7 + wdev,)), dma((7 + wdev,)),
            dma, dma((chunks,)), dma, dma((chunks,)), dma, dma((chunks,)),
        ],
        compiler_params=pltpu.CompilerParams(collective_id=0, has_side_effects=True, vmem_limit_bytes=38 * 2**20),
    )(*[pltpu.with_memory_space_constraint(each, pltpu.HBM)
        for each in (flat, walkers, inv, rot, full_chol, field_noise.reshape(1, group))])
    results = [pltpu.with_memory_space_constraint(result, pltpu.VMEM) for result in results]
    out, fb, shift = pl.pallas_call(
        closing,
        out_shape=(jax.ShapeDtypeStruct(flat.shape, bf16), jax.ShapeDtypeStruct((wdev, group), f32),
                   jax.ShapeDtypeStruct((1, group), f32)),
        in_specs=[vmem] * 5,
        out_specs=(hbm,) * 3,
        scratch_shapes=[pltpu.VMEM(flat.shape, bf16), dma((10,))],
        compiler_params=pltpu.CompilerParams(vmem_limit_bytes=16 * 2**20),
    )(*results)
    return (out.reshape(walkers.shape), fb, shift.reshape(group))


def solution(mesh):
    placed = (
        P(("blk", "walk"), None, None),
        P(("blk", "walk"), None, None, None),
        P("blk", None, None),
        P("walk", "blk", None),
        P(),
    )
    return jax.shard_map(
        functools.partial(local, mesh.shape["blk"], mesh.shape["walk"]),
        mesh=mesh,
        in_specs=placed,
        out_specs=(P(("blk", "walk"), None, None), P(("blk", "walk"), None), P()),
        check_vma=False,
    )
```

```python
import functools
import math

import jax
import jax.numpy as jnp
from jax import lax
from jax.experimental import pallas as pl
from jax.experimental.pallas import tpu as pltpu
from jax.sharding import PartitionSpec as P

time_root = 0.1
orders = 4
f32, bf16 = jnp.float32, jnp.bfloat16
MESH = pl.DeviceIdType.MESH


class Gather:
    def __init__(self, nb, ref_at, recv, send_f, send_s, send_w, send_b):
        self.nb, self.ref_at, self.recv = nb, ref_at, recv
        self.send_f, self.send_s, self.send_w, self.send_b = send_f, send_s, send_w, send_b
        me = lax.axis_index("blk")
        self.me, self.core = me, me % 2
        self.cols = 2 if nb % 4 == 0 else 1
        self.rows = nb // 2 // self.cols
        chip = me // 2
        col, row = chip % self.cols, chip // self.cols
        self.turn = self.core if self.rows == self.cols else 0
        self.f = (1 - self.turn) * col + self.turn * row
        self.s = (1 - self.turn) * row + self.turn * col
        self.nf, self.ns = self.cols, self.rows
        self.sibling = chip * 2 + 1 - self.core

    def at(self, i, j):
        f, s = (self.f + i) % self.nf, (self.s + j) % self.ns
        chip = (1 - self.turn) * (s * self.cols + f) + self.turn * (f * self.cols + s)
        return chip * 2 + self.core

    def copy(self, block, chunk, target, send):
        piece = self.ref_at(block, chunk)
        return pltpu.make_async_remote_copy(
            src_ref=piece, dst_ref=piece, send_sem=send, recv_sem=self.recv.at[block, chunk],
            device_id=target if isinstance(target, dict) else {"blk": target}, device_id_type=MESH)

    def landed(self, block, chunk):
        self.copy(block, chunk, self.sibling, self.send_b).wait_recv()

    def own(self, chunk):
        for i in range(1, self.nf):
            self.copy(self.me, chunk, self.at(i, 0), self.send_f).start()
        for j in range(1, self.ns):
            self.copy(self.me, chunk, self.at(0, j), self.send_s).start()
        self.copy(self.me, chunk, self.sibling, self.send_b).start()

    def first(self, chunk, forward):
        for i in range(1, self.nf):
            block = self.at(i, 0)
            self.landed(block, chunk)

            @pl.when(forward)
            def _():
                for j in range(1, self.ns):
                    self.copy(block, chunk, self.at(0, j), self.send_w).start()

            self.copy(block, chunk, self.sibling, self.send_b).start()

    def second(self, chunk, relayed):
        for j in range(1, self.ns):
            for i in range(self.nf):
                block = self.at(i, j)
                self.landed(block, chunk)
                if i and relayed is not None:
                    relayed(block)
                self.copy(block, chunk, self.sibling, self.send_b).start()


def kernel(nb, nw, total_walkers, chunks, parts, every, flat_hbm, three_hbm, inv_hbm, rot_hbm, full_hbm, noise_hbm,
           field, last, partial, fb, shift,
           flat, three, inv_raw, inv, noise, own_rot, rots, full, theta, thetas, pair, mine, zout, zin,
           vectors, spread_rows, wide, sums, fb_out, fb_in, mid, outer_in, inner_in, slots_w, slots_b, terms,
           fld_recv, fld_f, fld_s, fld_w, fld_b, fld_r,
           load, slot_send, slot_recv, in_send, in_recv, mid_send, mid_recv, out_send, out_recv):
    blk, walk = lax.axis_index("blk"), lax.axis_index("walk")
    wdev, occupied, orbitals = theta.shape
    per, tiles = rots.shape[3], rots.shape[2]
    group = nb * per
    slab = tiles * 128
    local_count, block_rows = full.shape[0], full.shape[1]
    size = orbitals // chunks

    loads = [pltpu.make_async_copy(src, dst, load.at[k]) for k, (src, dst) in enumerate((
        (inv_hbm, inv_raw), (three_hbm, three), (rot_hbm, own_rot), (noise_hbm, noise), (flat_hbm, flat), (full_hbm, full)))]
    for one in loads[:4]:
        one.start()
    load_inv, load_three, load_rot, load_noise, load_flat, load_full = loads
    barrier = pltpu.get_barrier_semaphore()
    for d in range(1, nb):
        pl.semaphore_signal(barrier, inc=1, device_id={"blk": (blk + d) % nb}, device_id_type=MESH)
    for d in range(1, nw):
        pl.semaphore_signal(barrier, inc=1, device_id={"walk": (walk + d) % nw}, device_id_type=MESH)

    def one_hot(shape, wanted):
        row, column = lax.broadcasted_iota(jnp.int32, shape, 0), lax.broadcasted_iota(jnp.int32, shape, 1)
        return jnp.where(wanted(row, column), 1.0, 0.0).astype(bf16)

    load_inv.wait()
    for w in range(wdev):
        whole = jnp.zeros((occupied, 2 * occupied), f32)
        for s in range(2):
            take = one_hot((occupied, inv_raw.shape[0]), lambda r, c: c == 2 * (r + w * occupied) + s)
            place = one_hot((occupied, 2 * occupied), lambda r, c: c == r + s * occupied)
            block = jnp.dot(take, inv_raw[...], preferred_element_type=f32).astype(bf16)
            whole = whole + jnp.dot(block, place, preferred_element_type=f32)
        inv[w] = whole.astype(bf16)
    for t in range(tiles):
        spread_rows[t] = one_hot(spread_rows.shape[1:],
                                 lambda r, c: (r >= (c * tiles + t) * per) & (r < (c * tiles + t + 1) * per))

    load_three.wait()
    load_rot.wait()
    for one in loads[4:]:
        one.start()
    pl.semaphore_wait(barrier, nb + nw - 2)

    def slab_of(b, z):
        return (b % 2) * nw + (b // 2 + z) % nw if parts == 2 else (b + z) % nw

    slab_columns = lambda s: pl.ds(pl.multiple_of(s * slab, slab), slab)
    home = slab_of(blk, walk)
    sibling = blk // 2 * 2 + 1 - blk % 2
    walk_peers = [({"walk": (walk + d) % nw}, (walk + d) % nw) for d in range(1, nw)]
    blk_peers = [({"blk": (blk + d) % nb}, (blk + d) % nb) for d in range(1, nb)]

    def share(slots, source_at, me, peers, k):
        for peer, slot in peers:
            pltpu.make_async_remote_copy(
                src_ref=source_at(slot), dst_ref=slots.at[me],
                send_sem=slot_send.at[k], recv_sem=slot_recv.at[k], device_id=peer, device_id_type=MESH).start()

        def finish():
            rest = slots.at[pl.ds(0, len(peers))]
            pltpu.make_async_remote_copy(
                src_ref=rest, dst_ref=rest, send_sem=slot_send.at[k], recv_sem=slot_recv.at[k],
                device_id=peers[0][0], device_id_type=MESH).wait()

        return finish

    rot_slab = lambda b: own_rot.at[:, pl.ds(slab_of(b, walk) * tiles, tiles)]
    rots_arrive = share(rots, rot_slab, blk, blk_peers, 0)
    keep_rot = pltpu.make_async_copy(rot_slab(blk), rots.at[blk], load.at[2])
    keep_rot.start()

    tile = 512
    span_width = mine.shape[1]

    def project(begin, into):
        for lo in range(0, span_width, tile):
            span = pl.ds(pl.multiple_of(begin + lo, tile), tile)
            both = jnp.zeros((occupied, tile), f32)
            for w in range(wdev):
                one = jnp.dot(inv[w], three[w, :, span], preferred_element_type=f32).astype(bf16)
                theta[w, :, span] = one
                both = both + one.astype(f32)
            into[:, lo:lo + tile] = both

    if parts == 2:
        project((1 - blk % 2) * span_width, pair.at[0])
        swap = pltpu.make_async_remote_copy(
            src_ref=pair.at[0], dst_ref=pair.at[1], send_sem=slot_send.at[4], recv_sem=slot_recv.at[4],
            device_id={"blk": sibling}, device_id_type=MESH)
        swap.start()
        project(blk % 2 * span_width, mine)
        swap.wait()
    else:
        project(0, mine)
    for k in range(nw):
        columns = slab_columns(slab_of(blk, k) % nw)
        value = mine[:, columns]
        if parts == 2:
            value = value + pair[1, :, columns]
        zout[k] = value.astype(bf16)
    zin[pl.ds(walk, 1)] = zout[pl.ds(walk, 1)]
    sums_arrive = share(zin, lambda z: zout.at[z], walk, walk_peers, 1)
    def send_thetas(w):
        return share(thetas.at[w], lambda b: theta.at[w, :, slab_columns(slab_of(b, walk))], blk, blk_peers,
                     2 if w == 0 else 6 + w)

    early = (wdev + 1) // 2
    thetas_arrive = [send_thetas(w) for w in range(early)]
    for w in range(wdev):
        thetas[w, pl.ds(blk, 1)] = theta[pl.ds(w, 1), :, slab_columns(home)]

    def widen(narrow):
        pieces = []
        for t in range(tiles):
            side = [each[:, t * 128:(t + 1) * 128] for each in narrow]
            side = side[0] if len(side) == 1 else jnp.concatenate(side, axis=1)
            pieces.append(jnp.dot(spread_rows[t], side, preferred_element_type=f32))
        return functools.reduce(jnp.add, pieces)

    deep = spread_rows.shape[1]
    fold = lambda value: jnp.sum(value.reshape(deep // 8, 8, 128), axis=0)
    row = lax.broadcasted_iota(jnp.int32, (nb * 8, 128), 0)
    lane = lax.broadcasted_iota(jnp.int32, (nb * 8, 128), 1)
    picked = lane == row // 8 * per + row % per

    def line_of(value):
        return jnp.sum(jnp.where(picked, jnp.sum(value, axis=1, keepdims=True), 0.0), axis=0, keepdims=True)

    keep_rot.wait()
    rots_arrive()
    for b in range(nb):
        vectors[b] = rots.at[b].reshape(deep, 128)[...].astype(f32)
    sums_arrive()
    value = zin[0].astype(f32)
    for k in range(1, nw):
        value = value + zin[k].astype(f32)
    wide[:, 0:128] = widen([value.astype(bf16)])
    for b in range(nb):
        sums[0, b * 8:(b + 1) * 8] = fold(vectors[b] * wide[:, 0:128])
    line = line_of(sums[0])
    for peers, me, slots, k in ((walk_peers, walk, slots_w, 5), (blk_peers, blk, slots_b, 6)):
        slots[pl.ds(me, 1)] = line[None]
        share(slots, lambda slot: slots.at[me], me, peers, k)()
        line = slots[0]
        for d in range(1, slots.shape[0]):
            line = line + slots[d]
    thetas_arrive += [send_thetas(w) for w in range(early, wdev)]
    shifts = line / math.sqrt(total_walkers)
    shift[...] = shifts[:, 0:group]
    load_noise.wait()
    shifted = (noise[...] - shifts[:, 0:group]) * time_root
    lanes = lax.broadcasted_iota(jnp.int32, (1, group), 1)
    weights = [jnp.sum(jnp.where(lanes == walk * local_count + j, shifted, 0.0), axis=1, keepdims=True)
               for j in range(local_count)]
    load_full.wait()
    load_flat.wait()

    half = nw // 2
    is_mid = (walk == half - 1) | (walk == half)
    has_outer = (walk != 0) & (walk != nw - 1)
    step = 1 - 2 * (walk >= half).astype(jnp.int32)
    inward = (walk + step + nw) % nw
    outward = (walk - step + nw) % nw
    outer_lag = min(12, chunks)
    lag = jnp.where(is_mid, 3, outer_lag)
    cols = lambda c: pl.ds(pl.multiple_of(c * size, size), size)
    rows = lambda block: pl.ds(pl.multiple_of(block * block_rows, block_rows), block_rows)
    part_at = lambda block, c: field.at[rows(block), cols(c)]
    gather = Gather(nb, part_at, fld_recv, fld_f, fld_s, fld_w, fld_b)

    def hop(src, dst, send, recv, target):
        return pltpu.make_async_remote_copy(src_ref=src, dst_ref=dst, send_sem=send, recv_sem=recv,
                                            device_id={"walk": target}, device_id_type=MESH)

    def to_mid(c):
        return hop(mid.at[c], outer_in.at[c], in_send, in_recv.at[c], inward)

    def across(c):
        return hop(mid.at[c], inner_in.at[c], mid_send, mid_recv.at[c], inward)

    def back(c):
        return hop(part_at(blk, c), part_at(blk, c), out_send, out_recv.at[c], outward)

    def reduce_in(c):
        value = weights[0] * full[0, :, cols(c)].astype(f32)
        for j in range(1, local_count):
            value = value + weights[j] * full[j, :, cols(c)].astype(f32)

        @pl.when(has_outer)
        def _():
            to_mid(c).wait_recv()
            mid[c] = (value + outer_in[c].astype(f32)).astype(bf16)

        @pl.when(jnp.logical_not(has_outer))
        def _():
            mid[c] = value.astype(bf16)

        @pl.when(is_mid)
        def _():
            across(c).start()

        @pl.when(jnp.logical_not(is_mid))
        def _():
            to_mid(c).start()

    def spread(c):
        @pl.when(is_mid)
        def _():
            across(c).wait_recv()
            field[rows(blk), cols(c)] = (mid[c].astype(f32) + inner_in[c].astype(f32)).astype(bf16)

        @pl.when(jnp.logical_not(is_mid))
        def _():
            back(c).wait_recv()

        @pl.when(has_outer)
        def _():
            back(c).start()

        gather.own(c)

    by_walk = lambda c: (c % 2 == 1) & (c < 10)
    relays = len([c for c in range(chunks) if c % 2 == 1 and c < 10]) if every else 0

    def first(c):
        gather.first(c, is_mid | jnp.logical_not(by_walk(c)) if every else c >= 0)

    def second(c):
        def relayed(block):
            @pl.when(is_mid & by_walk(c))
            def _():
                gather.copy(block, c, {"walk": outward}, fld_r).start()

        gather.second(c, relayed if every else None)

    def when_chunk(c, action):
        @pl.when((c >= 0) & (c < chunks))
        def _():
            action(c)

    def first_term(c):
        for e in range(2):
            for d in range(nb // 2):
                gather.landed((sibling + 2 * d) % nb, c - 1 + e)
        span = pl.ds(pl.multiple_of((c - 1) * size, 2 * size), 2 * size)
        terms[0, :, span] = jnp.dot(flat[...], field[:, span], preferred_element_type=f32).astype(bf16)

    def bias(b):
        wide[...] = widen([thetas[w, b] for w in range(wdev)])

        @pl.loop(0, nb)
        def _(v):
            for w in range(wdev):
                sums[w, pl.ds(pl.multiple_of(v * 8, 8), 8)] = fold(vectors[v] * wide[:, w * 128:(w + 1) * 128])

        for w in range(wdev):
            fb_out[b, w:w + 1] = line_of(sums[w])

    split = orbitals // 2
    ready = split // size - 1
    bias_start = jnp.where(is_mid, 6, outer_lag - 1)
    bias_pace = jnp.where(is_mid, 2 if nb <= 8 else 1, 4 * chunks)

    @pl.loop(0, chunks + outer_lag + 11)
    def _(t):
        when_chunk(t - lag, spread)
        when_chunk(t, reduce_in)
        when_chunk(t - lag - 3, first)
        when_chunk(t - lag - 9, second)
        @pl.when(t == bias_start)
        def _():
            for arrive in thetas_arrive:
                arrive()

        begin = (t - bias_start) // bias_pace

        @pl.when((t >= bias_start) & ((t - bias_start) % bias_pace == 0) & (begin < nb))
        def _():
            @pl.loop(jnp.where(is_mid, begin, 0), jnp.where(is_mid, begin + 1, nb))
            def _(b):
                bias(b)

        @pl.when(((t - lag - 10) % 2 == 1) & (t - lag - 10 > 0) & (t - lag - 10 < chunks))
        def _():
            first_term(t - lag - 10)

        piece = t - lag - 10 - ready

        @pl.when((piece >= 0) & (piece < split // tile))
        def _():
            span = pl.ds(pl.multiple_of(piece * tile, tile), tile)
            partial[:, span] = jnp.dot(terms[0, :, 0:split], field[0:split, span], preferred_element_type=f32)

    fb_in[pl.ds(blk, 1)] = fb_out[pl.ds(blk, 1)]
    biases_arrive = share(fb_in, lambda b: fb_out.at[b], blk, blk_peers, 3)

    for n in range(orbitals // tile):
        span = slice(n * tile, (n + 1) * tile)
        if n < split // tile:
            value = partial[:, span] + jnp.dot(terms[0, :, split:], field[split:, span], preferred_element_type=f32)
        else:
            value = jnp.dot(terms[0], field[:, span], preferred_element_type=f32)
        terms[1, :, span] = (value / 2).astype(bf16)

    width = orbitals // 2
    for order in range(3, orders):
        @pl.loop(0, orbitals // width)
        def _(n):
            span = pl.ds(pl.multiple_of(n * width, width), width)
            term = (jnp.dot(terms[order - 2], field[:, span], preferred_element_type=f32) / order).astype(bf16)
            if order == orders - 1:
                value = flat[:, span].astype(f32)
                for k in range(orders - 2):
                    value = value + terms[k, :, span].astype(f32)
                partial[:, span] = value + term.astype(f32)
                last[:, span] = term
            else:
                terms[order - 1, :, span] = term

    biases_arrive()
    value = fb_in[0]
    for b in range(1, nb):
        value = value + fb_in[b]
    fb[...] = value[:, 0:group]

    def drain(piece, send):
        pltpu.make_async_remote_copy(src_ref=piece, dst_ref=piece, send_sem=send, recv_sem=fld_recv.at[0, 0],
                                     device_id={"blk": sibling}, device_id_type=MESH).wait_send()

    def many(count, send):
        if count:
            drain(field.at[pl.ds(0, count * block_rows)], send)

    many(gather.nf - 1, fld_f)
    many(gather.ns - 1, fld_s)
    many(nb // 2, fld_b)
    if every:
        @pl.when(is_mid)
        def _():
            many((gather.ns - 1) * (gather.nf - 1), fld_w)
            drain(field.at[pl.ds(0, block_rows), pl.ds(0, relays * size)], fld_r)

        @pl.when(jnp.logical_not(is_mid))
        def _():
            drain(field.at[pl.ds(0, block_rows), pl.ds(0, (chunks - relays) * size)], fld_w)
    else:
        many((gather.ns - 1) * (gather.nf - 1), fld_w)

    @pl.when(is_mid)
    def _():
        drain(mid, mid_send)

    @pl.when(jnp.logical_not(is_mid))
    def _():
        drain(mid, in_send)

    @pl.when(has_outer)
    def _():
        drain(field.at[pl.ds(0, block_rows)], out_send)


def closing(field, last, partial, fb, shift, out, fb_out, shift_out, held, sems):
    orbitals = field.shape[1]
    width = orbitals // 8
    small = [pltpu.make_async_copy(src, dst, sems.at[8 + k]) for k, (src, dst) in enumerate(((fb, fb_out), (shift, shift_out)))]
    for copy in small:
        copy.start()
    copies = []
    for n in range(8):
        span = pl.ds(n * width, width)
        term = (jnp.dot(last[...], field[:, span], preferred_element_type=f32) / orders).astype(bf16)
        held[:, span] = (partial[:, span] + term.astype(f32)).astype(bf16)
        copies.append(pltpu.make_async_copy(held.at[:, span], out.at[:, span], sems.at[n]))
        copies[-1].start()
    for copy in small + copies:
        copy.wait()


def local(nb, nw, walkers, inv_intersection, rotated_chol, full_chol, field_noise):
    wdev, double_rows, orbitals = walkers.shape
    occupied = double_rows // 2
    group = field_noise.shape[0]
    per = rotated_chol.shape[0]
    local_count, block_rows, _ = full_chol.shape
    chunks = 16
    size = orbitals // chunks
    parts = nb // nw
    assert nb == parts * nw and parts in (1, 2)
    tiles = orbitals // nb // 128
    every = 3 if nw == 4 and nb == 8 else 0
    flat = walkers.reshape(wdev * double_rows, orbitals)
    inv = inv_intersection.transpose(0, 2, 1, 3).reshape(wdev * double_rows, occupied)
    rot = rotated_chol.transpose(1, 0, 2).reshape(occupied, per, orbitals // 128, 128).transpose(0, 2, 1, 3)
    vmem, hbm = pl.BlockSpec(memory_space=pltpu.VMEM), pl.BlockSpec(memory_space=pltpu.HBM)
    dma = pltpu.SemaphoreType.DMA
    span = orbitals // parts
    results = pl.pallas_call(
        functools.partial(kernel, nb, nw, wdev * nb * nw, chunks, parts, every),
        out_shape=(pltpu.VMEM((orbitals, orbitals), bf16), pltpu.VMEM(flat.shape, bf16), pltpu.VMEM(flat.shape, f32),
                   pltpu.VMEM((wdev, group), f32), pltpu.VMEM((1, group), f32)),
        in_specs=[hbm] * 6,
        out_specs=(vmem,) * 5,
        scratch_shapes=[
            pltpu.VMEM(flat.shape, bf16),
            pltpu.VMEM(walkers.shape, bf16),
            pltpu.VMEM(inv.shape, bf16),
            pltpu.VMEM((wdev, occupied, double_rows), bf16),
            pltpu.VMEM((1, group), f32),
            pltpu.VMEM(rot.shape, bf16),
            pltpu.VMEM((nb, occupied, tiles, per, 128), bf16),
            pltpu.VMEM(full_chol.shape, bf16),
            pltpu.VMEM((wdev, occupied, orbitals), bf16),
            pltpu.VMEM((wdev, nb, occupied, tiles * 128), bf16),
            pltpu.VMEM((2, occupied, span), f32),
            pltpu.VMEM((occupied, span), f32),
            pltpu.VMEM((nw, occupied, tiles * 128), bf16),
            pltpu.VMEM((nw, occupied, tiles * 128), bf16),
            pltpu.VMEM((nb, occupied * tiles * per, 128), f32),
            pltpu.VMEM((tiles, occupied * tiles * per, occupied), bf16),
            pltpu.VMEM((occupied * tiles * per, wdev * 128), f32),
            pltpu.VMEM((wdev, nb * 8, 128), f32),
            pltpu.VMEM((nb, wdev, 128), f32),
            pltpu.VMEM((nb, wdev, 128), f32),
            pltpu.VMEM((chunks, block_rows, size), bf16),
            pltpu.VMEM((chunks, block_rows, size), bf16),
            pltpu.VMEM((chunks, block_rows, size), bf16),
            pltpu.VMEM((nw, 1, 128), f32),
            pltpu.VMEM((nb, 1, 128), f32),
            pltpu.VMEM((orders - 2,) + flat.shape, bf16),
            dma((nb, chunks)), dma, dma, dma, dma, dma,
            dma((6,)), dma((7 + wdev,)), dma((7 + wdev,)),
            dma, dma((chunks,)), dma, dma((chunks,)), dma, dma((chunks,)),
        ],
        compiler_params=pltpu.CompilerParams(collective_id=0, has_side_effects=True, vmem_limit_bytes=38 * 2**20),
    )(*[pltpu.with_memory_space_constraint(each, pltpu.HBM)
        for each in (flat, walkers, inv, rot, full_chol, field_noise.reshape(1, group))])
    results = [pltpu.with_memory_space_constraint(result, pltpu.VMEM) for result in results]
    out, fb, shift = pl.pallas_call(
        closing,
        out_shape=(jax.ShapeDtypeStruct(flat.shape, bf16), jax.ShapeDtypeStruct((wdev, group), f32),
                   jax.ShapeDtypeStruct((1, group), f32)),
        in_specs=[vmem] * 5,
        out_specs=(hbm,) * 3,
        scratch_shapes=[pltpu.VMEM(flat.shape, bf16), dma((10,))],
        compiler_params=pltpu.CompilerParams(vmem_limit_bytes=16 * 2**20),
    )(*results)
    return (out.reshape(walkers.shape), fb, shift.reshape(group))


def solution(mesh):
    placed = (
        P(("blk", "walk"), None, None),
        P(("blk", "walk"), None, None, None),
        P("blk", None, None),
        P("walk", "blk", None),
        P(),
    )
    return jax.shard_map(
        functools.partial(local, mesh.shape["blk"], mesh.shape["walk"]),
        mesh=mesh,
        in_specs=placed,
        out_specs=(P(("blk", "walk"), None, None), P(("blk", "walk"), None), P()),
        check_vma=False,
    )
```

```python
import functools
import math

import jax
import jax.numpy as jnp
from jax import lax
from jax.experimental import pallas as pl
from jax.experimental.pallas import tpu as pltpu
from jax.sharding import PartitionSpec as P

time_root = 0.1
orders = 4
f32, bf16 = jnp.float32, jnp.bfloat16
MESH = pl.DeviceIdType.MESH


class Gather:
    def __init__(self, nb, ref_at, recv, send_f, send_s, send_w, send_b):
        self.nb, self.ref_at, self.recv = nb, ref_at, recv
        self.send_f, self.send_s, self.send_w, self.send_b = send_f, send_s, send_w, send_b
        me = lax.axis_index("blk")
        self.me, self.core = me, me % 2
        self.cols = 2 if nb % 4 == 0 else 1
        self.rows = nb // 2 // self.cols
        chip = me // 2
        col, row = chip % self.cols, chip // self.cols
        self.turn = self.core if self.rows == self.cols else 0
        self.f = (1 - self.turn) * col + self.turn * row
        self.s = (1 - self.turn) * row + self.turn * col
        self.nf, self.ns = self.cols, self.rows
        self.sibling = chip * 2 + 1 - self.core

    def at(self, i, j):
        f, s = (self.f + i) % self.nf, (self.s + j) % self.ns
        chip = (1 - self.turn) * (s * self.cols + f) + self.turn * (f * self.cols + s)
        return chip * 2 + self.core

    def copy(self, block, chunk, target, send):
        piece = self.ref_at(block, chunk)
        return pltpu.make_async_remote_copy(
            src_ref=piece, dst_ref=piece, send_sem=send, recv_sem=self.recv.at[block, chunk],
            device_id=target if isinstance(target, dict) else {"blk": target}, device_id_type=MESH)

    def landed(self, block, chunk):
        self.copy(block, chunk, self.sibling, self.send_b).wait_recv()

    def own(self, chunk):
        for i in range(1, self.nf):
            self.copy(self.me, chunk, self.at(i, 0), self.send_f).start()
        for j in range(1, self.ns):
            self.copy(self.me, chunk, self.at(0, j), self.send_s).start()
        self.copy(self.me, chunk, self.sibling, self.send_b).start()

    def first(self, chunk, forward):
        for i in range(1, self.nf):
            block = self.at(i, 0)
            self.landed(block, chunk)

            @pl.when(forward)
            def _():
                for j in range(1, self.ns):
                    self.copy(block, chunk, self.at(0, j), self.send_w).start()

            self.copy(block, chunk, self.sibling, self.send_b).start()

    def second(self, chunk, relayed):
        for j in range(1, self.ns):
            for i in range(self.nf):
                block = self.at(i, j)
                self.landed(block, chunk)
                if i and relayed is not None:
                    relayed(block)
                self.copy(block, chunk, self.sibling, self.send_b).start()


def kernel(nb, nw, total_walkers, chunks, parts, every, flat_hbm, three_hbm, inv_hbm, rot_hbm, full_hbm, noise_hbm,
           field, last, partial, fb, shift,
           flat, three, inv_raw, inv, noise, own_rot, rots, full, theta, thetas, pair, mine, zout, zin,
           vectors, spread_rows, wide, sums, fb_out, fb_in, mid, outer_in, inner_in, slots_w, slots_b, terms,
           fld_recv, fld_f, fld_s, fld_w, fld_b, fld_r,
           load, slot_send, slot_recv, in_send, in_recv, mid_send, mid_recv, out_send, out_recv):
    blk, walk = lax.axis_index("blk"), lax.axis_index("walk")
    wdev, occupied, orbitals = theta.shape
    per, tiles = rots.shape[3], rots.shape[2]
    group = nb * per
    slab = tiles * 128
    local_count, block_rows = full.shape[0], full.shape[1]
    size = orbitals // chunks

    loads = [pltpu.make_async_copy(src, dst, load.at[k]) for k, (src, dst) in enumerate((
        (inv_hbm, inv_raw), (three_hbm, three), (rot_hbm, own_rot), (noise_hbm, noise), (flat_hbm, flat), (full_hbm, full)))]
    for one in loads[:4]:
        one.start()
    load_inv, load_three, load_rot, load_noise, load_flat, load_full = loads
    barrier = pltpu.get_barrier_semaphore()
    for d in range(1, nb):
        pl.semaphore_signal(barrier, inc=1, device_id={"blk": (blk + d) % nb}, device_id_type=MESH)
    for d in range(1, nw):
        pl.semaphore_signal(barrier, inc=1, device_id={"walk": (walk + d) % nw}, device_id_type=MESH)

    def one_hot(shape, wanted):
        row, column = lax.broadcasted_iota(jnp.int32, shape, 0), lax.broadcasted_iota(jnp.int32, shape, 1)
        return jnp.where(wanted(row, column), 1.0, 0.0).astype(bf16)

    load_inv.wait()
    for w in range(wdev):
        whole = jnp.zeros((occupied, 2 * occupied), f32)
        for s in range(2):
            take = one_hot((occupied, inv_raw.shape[0]), lambda r, c: c == 2 * (r + w * occupied) + s)
            place = one_hot((occupied, 2 * occupied), lambda r, c: c == r + s * occupied)
            block = jnp.dot(take, inv_raw[...], preferred_element_type=f32).astype(bf16)
            whole = whole + jnp.dot(block, place, preferred_element_type=f32)
        inv[w] = whole.astype(bf16)
    for t in range(tiles):
        spread_rows[t] = one_hot(spread_rows.shape[1:],
                                 lambda r, c: (r >= (c * tiles + t) * per) & (r < (c * tiles + t + 1) * per))

    load_three.wait()
    load_rot.wait()
    for one in loads[4:]:
        one.start()
    pl.semaphore_wait(barrier, nb + nw - 2)

    def slab_of(b, z):
        return (b % 2) * nw + (b // 2 + z) % nw if parts == 2 else (b + z) % nw

    slab_columns = lambda s: pl.ds(pl.multiple_of(s * slab, slab), slab)
    home = slab_of(blk, walk)
    sibling = blk // 2 * 2 + 1 - blk % 2
    walk_peers = [({"walk": (walk + d) % nw}, (walk + d) % nw) for d in range(1, nw)]
    blk_peers = [({"blk": (blk + d) % nb}, (blk + d) % nb) for d in range(1, nb)]

    def share(slots, source_at, me, peers, k):
        for peer, slot in peers:
            pltpu.make_async_remote_copy(
                src_ref=source_at(slot), dst_ref=slots.at[me],
                send_sem=slot_send.at[k], recv_sem=slot_recv.at[k], device_id=peer, device_id_type=MESH).start()

        def finish():
            rest = slots.at[pl.ds(0, len(peers))]
            pltpu.make_async_remote_copy(
                src_ref=rest, dst_ref=rest, send_sem=slot_send.at[k], recv_sem=slot_recv.at[k],
                device_id=peers[0][0], device_id_type=MESH).wait()

        return finish

    rot_slab = lambda b: own_rot.at[:, pl.ds(slab_of(b, walk) * tiles, tiles)]
    rots_arrive = share(rots, rot_slab, blk, blk_peers, 0)
    keep_rot = pltpu.make_async_copy(rot_slab(blk), rots.at[blk], load.at[2])
    keep_rot.start()

    tile = 512
    span_width = mine.shape[1]

    def project(begin, into):
        for lo in range(0, span_width, tile):
            span = pl.ds(pl.multiple_of(begin + lo, tile), tile)
            both = jnp.zeros((occupied, tile), f32)
            for w in range(wdev):
                one = jnp.dot(inv[w], three[w, :, span], preferred_element_type=f32).astype(bf16)
                theta[w, :, span] = one
                both = both + one.astype(f32)
            into[:, lo:lo + tile] = both

    if parts == 2:
        project((1 - blk % 2) * span_width, pair.at[0])
        swap = pltpu.make_async_remote_copy(
            src_ref=pair.at[0], dst_ref=pair.at[1], send_sem=slot_send.at[4], recv_sem=slot_recv.at[4],
            device_id={"blk": sibling}, device_id_type=MESH)
        swap.start()
        project(blk % 2 * span_width, mine)
        swap.wait()
    else:
        project(0, mine)
    for k in range(nw):
        columns = slab_columns(slab_of(blk, k) % nw)
        value = mine[:, columns]
        if parts == 2:
            value = value + pair[1, :, columns]
        zout[k] = value.astype(bf16)
    zin[pl.ds(walk, 1)] = zout[pl.ds(walk, 1)]
    sums_arrive = share(zin, lambda z: zout.at[z], walk, walk_peers, 1)
    def send_thetas(w):
        return share(thetas.at[w], lambda b: theta.at[w, :, slab_columns(slab_of(b, walk))], blk, blk_peers,
                     2 if w == 0 else 6 + w)

    early = (wdev + 1) // 2
    thetas_arrive = [send_thetas(w) for w in range(early)]
    for w in range(wdev):
        thetas[w, pl.ds(blk, 1)] = theta[pl.ds(w, 1), :, slab_columns(home)]

    def widen(narrow):
        pieces = []
        for t in range(tiles):
            side = [each[:, t * 128:(t + 1) * 128] for each in narrow]
            side = side[0] if len(side) == 1 else jnp.concatenate(side, axis=1)
            pieces.append(jnp.dot(spread_rows[t], side, preferred_element_type=f32))
        return functools.reduce(jnp.add, pieces)

    deep = spread_rows.shape[1]
    fold = lambda value: jnp.sum(value.reshape(deep // 8, 8, 128), axis=0)
    row = lax.broadcasted_iota(jnp.int32, (nb * 8, 128), 0)
    lane = lax.broadcasted_iota(jnp.int32, (nb * 8, 128), 1)
    picked = lane == row // 8 * per + row % per

    def line_of(value):
        return jnp.sum(jnp.where(picked, jnp.sum(value, axis=1, keepdims=True), 0.0), axis=0, keepdims=True)

    keep_rot.wait()
    rots_arrive()
    for b in range(nb):
        vectors[b] = rots.at[b].reshape(deep, 128)[...].astype(f32)
    sums_arrive()
    value = zin[0].astype(f32)
    for k in range(1, nw):
        value = value + zin[k].astype(f32)
    wide[:, 0:128] = widen([value.astype(bf16)])
    for b in range(nb):
        sums[0, b * 8:(b + 1) * 8] = fold(vectors[b] * wide[:, 0:128])
    line = line_of(sums[0])
    for peers, me, slots, k in ((walk_peers, walk, slots_w, 5), (blk_peers, blk, slots_b, 6)):
        slots[pl.ds(me, 1)] = line[None]
        share(slots, lambda slot: slots.at[me], me, peers, k)()
        line = slots[0]
        for d in range(1, slots.shape[0]):
            line = line + slots[d]
    thetas_arrive += [send_thetas(w) for w in range(early, wdev)]
    shifts = line / math.sqrt(total_walkers)
    shift[...] = shifts[:, 0:group]
    load_noise.wait()
    shifted = (noise[...] - shifts[:, 0:group]) * time_root
    lanes = lax.broadcasted_iota(jnp.int32, (1, group), 1)
    weights = [jnp.sum(jnp.where(lanes == walk * local_count + j, shifted, 0.0), axis=1, keepdims=True)
               for j in range(local_count)]
    load_full.wait()
    load_flat.wait()

    half = nw // 2
    is_mid = (walk == half - 1) | (walk == half)
    has_outer = (walk != 0) & (walk != nw - 1)
    step = 1 - 2 * (walk >= half).astype(jnp.int32)
    inward = (walk + step + nw) % nw
    outward = (walk - step + nw) % nw
    outer_lag = min(12, chunks)
    lag = jnp.where(is_mid, 3, outer_lag)
    cols = lambda c: pl.ds(pl.multiple_of(c * size, size), size)
    rows = lambda block: pl.ds(pl.multiple_of(block * block_rows, block_rows), block_rows)
    part_at = lambda block, c: field.at[rows(block), cols(c)]
    gather = Gather(nb, part_at, fld_recv, fld_f, fld_s, fld_w, fld_b)

    def hop(src, dst, send, recv, target):
        return pltpu.make_async_remote_copy(src_ref=src, dst_ref=dst, send_sem=send, recv_sem=recv,
                                            device_id={"walk": target}, device_id_type=MESH)

    def to_mid(c):
        return hop(mid.at[c], outer_in.at[c], in_send, in_recv.at[c], inward)

    def across(c):
        return hop(mid.at[c], inner_in.at[c], mid_send, mid_recv.at[c], inward)

    def back(c):
        return hop(part_at(blk, c), part_at(blk, c), out_send, out_recv.at[c], outward)

    def reduce_in(c):
        value = weights[0] * full[0, :, cols(c)].astype(f32)
        for j in range(1, local_count):
            value = value + weights[j] * full[j, :, cols(c)].astype(f32)

        @pl.when(has_outer)
        def _():
            to_mid(c).wait_recv()
            mid[c] = (value + outer_in[c].astype(f32)).astype(bf16)

        @pl.when(jnp.logical_not(has_outer))
        def _():
            mid[c] = value.astype(bf16)

        @pl.when(is_mid)
        def _():
            across(c).start()

        @pl.when(jnp.logical_not(is_mid))
        def _():
            to_mid(c).start()

    def spread(c):
        @pl.when(is_mid)
        def _():
            across(c).wait_recv()
            field[rows(blk), cols(c)] = (mid[c].astype(f32) + inner_in[c].astype(f32)).astype(bf16)

        @pl.when(jnp.logical_not(is_mid))
        def _():
            back(c).wait_recv()

        @pl.when(has_outer)
        def _():
            back(c).start()

        gather.own(c)

    by_walk = lambda c: (c % 2 == 1) & (c < 12)
    relays = len([c for c in range(chunks) if c % 2 == 1 and c < 12]) if every else 0

    def first(c):
        gather.first(c, is_mid | jnp.logical_not(by_walk(c)) if every else c >= 0)

    def second(c):
        def relayed(block):
            @pl.when(is_mid & by_walk(c))
            def _():
                gather.copy(block, c, {"walk": outward}, fld_r).start()

        gather.second(c, relayed if every else None)

    def when_chunk(c, action):
        @pl.when((c >= 0) & (c < chunks))
        def _():
            action(c)

    def first_term(c):
        for e in range(2):
            for d in range(nb // 2):
                gather.landed((sibling + 2 * d) % nb, c - 1 + e)
        span = pl.ds(pl.multiple_of((c - 1) * size, 2 * size), 2 * size)
        terms[0, :, span] = jnp.dot(flat[...], field[:, span], preferred_element_type=f32).astype(bf16)

    def bias(b):
        wide[...] = widen([thetas[w, b] for w in range(wdev)])

        @pl.loop(0, nb)
        def _(v):
            for w in range(wdev):
                sums[w, pl.ds(pl.multiple_of(v * 8, 8), 8)] = fold(vectors[v] * wide[:, w * 128:(w + 1) * 128])

        for w in range(wdev):
            fb_out[b, w:w + 1] = line_of(sums[w])

    split = orbitals // 2
    ready = split // size - 1
    bias_start = jnp.where(is_mid, 6, outer_lag - 1)
    bias_pace = jnp.where(is_mid, 2 if nb <= 8 else 1, 4 * chunks)

    @pl.loop(0, chunks + outer_lag + 11)
    def _(t):
        when_chunk(t - lag, spread)
        when_chunk(t, reduce_in)
        when_chunk(t - lag - 3, first)
        when_chunk(t - lag - 9, second)
        @pl.when(t == bias_start)
        def _():
            for arrive in thetas_arrive:
                arrive()

        begin = (t - bias_start) // bias_pace

        @pl.when((t >= bias_start) & ((t - bias_start) % bias_pace == 0) & (begin < nb))
        def _():
            @pl.loop(jnp.where(is_mid, begin, 0), jnp.where(is_mid, begin + 1, nb))
            def _(b):
                bias(b)

        @pl.when(((t - lag - 10) % 2 == 1) & (t - lag - 10 > 0) & (t - lag - 10 < chunks))
        def _():
            first_term(t - lag - 10)

        piece = t - lag - 10 - ready

        @pl.when((piece >= 0) & (piece < split // tile))
        def _():
            span = pl.ds(pl.multiple_of(piece * tile, tile), tile)
            partial[:, span] = jnp.dot(terms[0, :, 0:split], field[0:split, span], preferred_element_type=f32)

    fb_in[pl.ds(blk, 1)] = fb_out[pl.ds(blk, 1)]
    biases_arrive = share(fb_in, lambda b: fb_out.at[b], blk, blk_peers, 3)

    for n in range(orbitals // tile):
        span = slice(n * tile, (n + 1) * tile)
        if n < split // tile:
            value = partial[:, span] + jnp.dot(terms[0, :, split:], field[split:, span], preferred_element_type=f32)
        else:
            value = jnp.dot(terms[0], field[:, span], preferred_element_type=f32)
        terms[1, :, span] = (value / 2).astype(bf16)

    width = orbitals // 2
    for order in range(3, orders):
        @pl.loop(0, orbitals // width)
        def _(n):
            span = pl.ds(pl.multiple_of(n * width, width), width)
            term = (jnp.dot(terms[order - 2], field[:, span], preferred_element_type=f32) / order).astype(bf16)
            if order == orders - 1:
                value = flat[:, span].astype(f32)
                for k in range(orders - 2):
                    value = value + terms[k, :, span].astype(f32)
                partial[:, span] = value + term.astype(f32)
                last[:, span] = term
            else:
                terms[order - 1, :, span] = term

    biases_arrive()
    value = fb_in[0]
    for b in range(1, nb):
        value = value + fb_in[b]
    fb[...] = value[:, 0:group]

    def drain(piece, send):
        pltpu.make_async_remote_copy(src_ref=piece, dst_ref=piece, send_sem=send, recv_sem=fld_recv.at[0, 0],
                                     device_id={"blk": sibling}, device_id_type=MESH).wait_send()

    def many(count, send):
        if count:
            drain(field.at[pl.ds(0, count * block_rows)], send)

    many(gather.nf - 1, fld_f)
    many(gather.ns - 1, fld_s)
    many(nb // 2, fld_b)
    if every:
        @pl.when(is_mid)
        def _():
            many((gather.ns - 1) * (gather.nf - 1), fld_w)
            drain(field.at[pl.ds(0, block_rows), pl.ds(0, relays * size)], fld_r)

        @pl.when(jnp.logical_not(is_mid))
        def _():
            drain(field.at[pl.ds(0, block_rows), pl.ds(0, (chunks - relays) * size)], fld_w)
    else:
        many((gather.ns - 1) * (gather.nf - 1), fld_w)

    @pl.when(is_mid)
    def _():
        drain(mid, mid_send)

    @pl.when(jnp.logical_not(is_mid))
    def _():
        drain(mid, in_send)

    @pl.when(has_outer)
    def _():
        drain(field.at[pl.ds(0, block_rows)], out_send)


def closing(field, last, partial, fb, shift, out, fb_out, shift_out, held, sems):
    orbitals = field.shape[1]
    width = orbitals // 8
    small = [pltpu.make_async_copy(src, dst, sems.at[8 + k]) for k, (src, dst) in enumerate(((fb, fb_out), (shift, shift_out)))]
    for copy in small:
        copy.start()
    copies = []
    for n in range(8):
        span = pl.ds(n * width, width)
        term = (jnp.dot(last[...], field[:, span], preferred_element_type=f32) / orders).astype(bf16)
        held[:, span] = (partial[:, span] + term.astype(f32)).astype(bf16)
        copies.append(pltpu.make_async_copy(held.at[:, span], out.at[:, span], sems.at[n]))
        copies[-1].start()
    for copy in small + copies:
        copy.wait()


def local(nb, nw, walkers, inv_intersection, rotated_chol, full_chol, field_noise):
    wdev, double_rows, orbitals = walkers.shape
    occupied = double_rows // 2
    group = field_noise.shape[0]
    per = rotated_chol.shape[0]
    local_count, block_rows, _ = full_chol.shape
    chunks = 16
    size = orbitals // chunks
    parts = nb // nw
    assert nb == parts * nw and parts in (1, 2)
    tiles = orbitals // nb // 128
    every = 3 if nw == 4 and nb == 8 else 0
    flat = walkers.reshape(wdev * double_rows, orbitals)
    inv = inv_intersection.transpose(0, 2, 1, 3).reshape(wdev * double_rows, occupied)
    rot = rotated_chol.transpose(1, 0, 2).reshape(occupied, per, orbitals // 128, 128).transpose(0, 2, 1, 3)
    vmem, hbm = pl.BlockSpec(memory_space=pltpu.VMEM), pl.BlockSpec(memory_space=pltpu.HBM)
    dma = pltpu.SemaphoreType.DMA
    span = orbitals // parts
    results = pl.pallas_call(
        functools.partial(kernel, nb, nw, wdev * nb * nw, chunks, parts, every),
        out_shape=(pltpu.VMEM((orbitals, orbitals), bf16), pltpu.VMEM(flat.shape, bf16), pltpu.VMEM(flat.shape, f32),
                   pltpu.VMEM((wdev, group), f32), pltpu.VMEM((1, group), f32)),
        in_specs=[hbm] * 6,
        out_specs=(vmem,) * 5,
        scratch_shapes=[
            pltpu.VMEM(flat.shape, bf16),
            pltpu.VMEM(walkers.shape, bf16),
            pltpu.VMEM(inv.shape, bf16),
            pltpu.VMEM((wdev, occupied, double_rows), bf16),
            pltpu.VMEM((1, group), f32),
            pltpu.VMEM(rot.shape, bf16),
            pltpu.VMEM((nb, occupied, tiles, per, 128), bf16),
            pltpu.VMEM(full_chol.shape, bf16),
            pltpu.VMEM((wdev, occupied, orbitals), bf16),
            pltpu.VMEM((wdev, nb, occupied, tiles * 128), bf16),
            pltpu.VMEM((2, occupied, span), f32),
            pltpu.VMEM((occupied, span), f32),
            pltpu.VMEM((nw, occupied, tiles * 128), bf16),
            pltpu.VMEM((nw, occupied, tiles * 128), bf16),
            pltpu.VMEM((nb, occupied * tiles * per, 128), f32),
            pltpu.VMEM((tiles, occupied * tiles * per, occupied), bf16),
            pltpu.VMEM((occupied * tiles * per, wdev * 128), f32),
            pltpu.VMEM((wdev, nb * 8, 128), f32),
            pltpu.VMEM((nb, wdev, 128), f32),
            pltpu.VMEM((nb, wdev, 128), f32),
            pltpu.VMEM((chunks, block_rows, size), bf16),
            pltpu.VMEM((chunks, block_rows, size), bf16),
            pltpu.VMEM((chunks, block_rows, size), bf16),
            pltpu.VMEM((nw, 1, 128), f32),
            pltpu.VMEM((nb, 1, 128), f32),
            pltpu.VMEM((orders - 2,) + flat.shape, bf16),
            dma((nb, chunks)), dma, dma, dma, dma, dma,
            dma((6,)), dma((7 + wdev,)), dma((7 + wdev,)),
            dma, dma((chunks,)), dma, dma((chunks,)), dma, dma((chunks,)),
        ],
        compiler_params=pltpu.CompilerParams(collective_id=0, has_side_effects=True, vmem_limit_bytes=38 * 2**20),
    )(*[pltpu.with_memory_space_constraint(each, pltpu.HBM)
        for each in (flat, walkers, inv, rot, full_chol, field_noise.reshape(1, group))])
    results = [pltpu.with_memory_space_constraint(result, pltpu.VMEM) for result in results]
    out, fb, shift = pl.pallas_call(
        closing,
        out_shape=(jax.ShapeDtypeStruct(flat.shape, bf16), jax.ShapeDtypeStruct((wdev, group), f32),
                   jax.ShapeDtypeStruct((1, group), f32)),
        in_specs=[vmem] * 5,
        out_specs=(hbm,) * 3,
        scratch_shapes=[pltpu.VMEM(flat.shape, bf16), dma((10,))],
        compiler_params=pltpu.CompilerParams(vmem_limit_bytes=16 * 2**20),
    )(*results)
    return (out.reshape(walkers.shape), fb, shift.reshape(group))


def solution(mesh):
    placed = (
        P(("blk", "walk"), None, None),
        P(("blk", "walk"), None, None, None),
        P("blk", None, None),
        P("walk", "blk", None),
        P(),
    )
    return jax.shard_map(
        functools.partial(local, mesh.shape["blk"], mesh.shape["walk"]),
        mesh=mesh,
        in_specs=placed,
        out_specs=(P(("blk", "walk"), None, None), P(("blk", "walk"), None), P()),
        check_vma=False,
    )
```
